256 devices in a mesh: grp: 4 (over z_lo), row: 8 (over z_hi, y), col: 8 (over x, core).
Axes of the slice: x: 4, y: 4, z: 8 (z_hi: 2, z_lo: 4; z = z_hi * 4 + z_lo), core: 2. Of those that a mesh axis runs over, the one named last changes fastest.
Arguments:
- amplitudes: bfloat16 [1024, 16384], P(('grp', 'row'), 'col'), may hold values from -6 to 6
- ladder_ints: bfloat16 [16384, 16384], P('col', ('grp', 'row')), may hold values from -0.0625 to 0.0625
- tile_live: int32 [128, 128], P('col', ('grp', 'row')), may hold values 0 or 1
- cycle_direct: bfloat16 [4096, 4096], P('col', ('grp', 'row')), may hold values from -0.0625 to 0.0625
- cycle_exchange: bfloat16 [4096, 4096], P('col', ('grp', 'row')), may hold values from -0.0625 to 0.0625
- eps_occ: float32 [32], replicated, may hold values from -2 to -0.5
- eps_vir: float32 [128], replicated, may hold values from 0.5 to 3
Outputs:
- update: bfloat16 [1024, 16384], P('col', ('grp', 'row'))
The draws below stay inside these ranges and needn't reach their ends.
All inputs are finite; a program needn't handle non-finite values. No bound on the sum of `tile_live` on one device may be relied on, other than what follows from the above.
Results may differ from the reference program's by a relative error of at most 0.001.
Values may be sent and summed in bfloat16 or wider, within the bound.
No kernel may reach another device: no remote copies, remote signals or barrier semaphores. Data moves between devices by JAX's collectives and lax.ppermute only.
A program may use at most 64 MiB of HBM per device.

```python
import jax
import jax.numpy as jnp

OCC = 32
VIR = 128
TILE = 128
OP = 1024
VP = 16384
PH = 4096


def place_ends(drawn, rng, smallest, high):
    shape = drawn.shape
    spot = [jax.random.randint(jax.random.fold_in(rng, axis), (), 0, shape[axis]) for axis in range(len(shape))]
    drawn = drawn.at[tuple(spot)].set(smallest)
    longest = shape.index(max(shape))
    spot[longest] = (spot[longest] + 1) % shape[longest]
    return drawn.at[tuple(spot)].set(high)


def block_levels(key, dims, pieces, low, high):
    def one(axis_at, blocks):
        heights = jax.random.uniform(jax.random.fold_in(jax.random.fold_in(key, 6), axis_at), (blocks,), jnp.float32, low / len(pieces), high / len(pieces))
        return jnp.repeat(jnp.exp(heights), dims[axis_at] // blocks).reshape((-1,) + (1,) * (len(dims) - axis_at - 1))

    factor_of = one(*pieces[0])
    for cut in pieces[1:]:
        factor_of = factor_of * one(*cut)
    return factor_of


def bell_draw(own_key, shape, width, bound, shards=(), held_as=jnp.bfloat16):
    drawn = width * jax.random.normal(own_key, shape, jnp.float32)
    if shards:
        drawn = drawn * block_levels(own_key, shape, shards, -0.22, 0.18)
    return jnp.clip(drawn, -bound, bound).astype(held_as)


def setup_inputs(seed: int = 0) -> dict:
    seeds = jax.random.split(jax.random.key(seed), 8)
    amplitudes = bell_draw(seeds[0], (OP, VP), 1.0, 6.0, ((0, 32), (1, 8)))
    ladder_ints = bell_draw(seeds[1], (VP, VP), (VP // 2) ** -0.5, 0.0625, ((0, 8), (1, 32)))
    tile_live = place_ends((jax.random.randint(seeds[2], (VP // TILE, VP // TILE), 0, 2) < 1).astype(jnp.int32), jax.random.fold_in(seeds[2], 1), 0, 1)
    cycle_direct = bell_draw(seeds[3], (PH, PH), (2 * PH) ** -0.5, 0.0625, ((0, 8), (1, 32)))
    cycle_exchange = bell_draw(seeds[4], (PH, PH), (2 * PH) ** -0.5, 0.0625, ((0, 8), (1, 32)))
    eps_occ = jnp.clip(jax.random.uniform(seeds[5], (OCC,), jnp.float32, -2.0, -0.5), -2.0, -0.5)
    eps_vir = jnp.clip(jax.random.uniform(seeds[6], (VIR,), jnp.float32, 0.5, 3.0), 0.5, 3.0)
    return {"amplitudes": amplitudes, "ladder_ints": ladder_ints, "tile_live": tile_live, "cycle_direct": cycle_direct, "cycle_exchange": cycle_exchange, "eps_occ": eps_occ, "eps_vir": eps_vir}


def reference(amplitudes, ladder_ints, tile_live, cycle_direct, cycle_exchange, eps_occ, eps_vir):
    expanded = jnp.repeat(jnp.repeat(tile_live, TILE, axis=0), TILE, axis=1).astype(jnp.bfloat16)
    masked = ladder_ints * expanded
    ladder = jnp.dot(amplitudes, masked, preferred_element_type=jnp.float32)
    amp_four = amplitudes.reshape(OCC, OCC, VIR, VIR)
    u_one = amp_four.transpose(0, 2, 1, 3).reshape(PH, PH)
    u_two = amp_four.transpose(0, 3, 1, 2).reshape(PH, PH)
    cycle = jnp.dot(cycle_direct, u_one, preferred_element_type=jnp.float32)
    cycle = cycle + jnp.dot(cycle_exchange, u_two, preferred_element_type=jnp.float32)
    cycle_pairs = cycle.reshape(OCC, VIR, OCC, VIR).transpose(0, 2, 1, 3).reshape(OP, VP)
    denom = (eps_vir[None, None, :, None] + eps_vir[None, None, None, :]
             - eps_occ[:, None, None, None] - eps_occ[None, :, None, None]).reshape(OP, VP)
    return ((ladder + cycle_pairs) / denom).astype(jnp.bfloat16)
```

```python
import jax
import jax.numpy as jnp
from jax import lax
from jax.sharding import Mesh, PartitionSpec as P

G = ("zl", "zh", "y")
C = ("x", "core")
Z = ("zl", "zh")


def shift(n, s):
    return [(i, (i + s) % n) for i in range(n)]


def z_shift(s):
    at = lambda z: (z % 4) * 2 + z // 4
    return [(at(z), at((z + s) % 8)) for z in range(8)]


def gather_pairs(t):
    z0 = lax.axis_index("zh") * 4 + lax.axis_index("zl")
    y0 = lax.axis_index("y")
    parts = [(0, t)]
    fwd = bwd = t
    for k in range(1, 5):
        fwd = lax.ppermute(fwd, Z, z_shift(1))
        parts.append((-k, fwd))
        if k < 4:
            bwd = lax.ppermute(bwd, Z, z_shift(-1))
            parts.append((k, bwd))
    mine = jnp.zeros((8,) + t.shape, t.dtype)
    for d, part in parts:
        z = (z0 + (d & 7)) & 7
        mine = lax.dynamic_update_slice(mine, part[None], ((z & 3) * 2 + (z >> 2), 0, 0))
    whole = jnp.zeros((8, 4) + t.shape, t.dtype)
    whole = lax.dynamic_update_slice(whole, mine[:, None], (0, y0, 0, 0))
    for s in range(1, 4):
        got = lax.ppermute(mine, "y", shift(4, s))
        whole = lax.dynamic_update_slice(whole, got[:, None], (0, (y0 + 4 - s) & 3, 0, 0))
    return whole.reshape((32,) + t.shape)


def scatter_sum(p):
    x0 = lax.axis_index("x")
    c0 = lax.axis_index("core")
    p = p.reshape(4, 2, 128, 512)
    away = lax.dynamic_slice_in_dim(p, 1 - c0, 1, 1)
    got = lax.ppermute(away, "core", shift(2, 1))
    p = (lax.dynamic_slice_in_dim(p, c0, 1, 1) + got)[:, 0]
    out = lax.dynamic_slice_in_dim(p, x0, 1, 0)
    for s in (1, 3, 2):
        block = lax.dynamic_slice_in_dim(p, (x0 + s) & 3, 1, 0)
        out = out + lax.ppermute(block, "x", shift(4, s))
    return out[0]


def local(amplitudes, ladder_ints, tile_live, cycle_direct, cycle_exchange, eps_occ, eps_vir):
    occ, vir = 32, 128
    col = lax.axis_index(C)
    g = lax.axis_index(G)
    both = jnp.stack([cycle_direct, cycle_exchange]).reshape(2, 4, 32, 4, vir)
    both = both.transpose(2, 0, 1, 3, 4)
    both = lax.all_to_all(both, G, 0, 0, tiled=True)
    w = both[:, 0].reshape(512, vir).T.reshape(8, 16, 512)
    w = lax.all_to_all(w, C, 0, 0, tiled=True)
    w = w.reshape(8, 16, occ, 4, 4)
    x = lax.all_gather(both[:, 1], C, axis=0, tiled=False)
    t = gather_pairs(amplitudes)
    expanded = jnp.repeat(jnp.repeat(tile_live, 128, axis=0), 128, axis=1).astype(jnp.bfloat16)
    ladder = jnp.dot(t.reshape(1024, 2048), ladder_ints * expanded, preferred_element_type=jnp.float32)
    four = t.reshape(occ, occ, 16, vir)
    wm = w.transpose(0, 3, 4, 2, 1).reshape(128, 512)
    u1 = four.transpose(0, 2, 1, 3).reshape(512, occ * vir)
    one = jnp.dot(wm, u1, preferred_element_type=jnp.float32).reshape(occ, 4, occ, vir)
    xm = x.transpose(0, 2, 3, 1, 4).reshape(128, occ * vir)
    two = lax.dot_general(
        xm.reshape(128, occ, vir), four, (((1, 2), (0, 3)), ((), ())), preferred_element_type=jnp.float32
    ).reshape(occ, 4, occ, 16)
    one = lax.dynamic_update_slice_in_dim(
        one, lax.dynamic_slice_in_dim(one, col * 16, 16, 3) + two, col * 16, 3
    )
    part = ladder + one.transpose(0, 2, 1, 3).reshape(1024, 512)
    total = scatter_sum(part.reshape(8, 128, 512))
    occ_local = lax.dynamic_slice_in_dim(eps_occ, col * 4, 4)
    vir_local = lax.dynamic_slice_in_dim(eps_vir, g * 4, 4)
    denom = (
        vir_local[None, None, :, None]
        + eps_vir[None, None, None, :]
        - occ_local[:, None, None, None]
        - eps_occ[None, :, None, None]
    ).reshape(128, 512)
    return (total / denom).astype(jnp.bfloat16)


def solution(mesh):
    fine = Mesh(mesh.devices.reshape(4, 2, 4, 4, 2), ("zl", "zh", "y", "x", "core"))
    placed = (P(G, C), P(C, G), P(C, G), P(C, G), P(C, G), P(), P())
    return jax.shard_map(local, mesh=fine, in_specs=placed, out_specs=P(C, G), check_vma=False)
```

```python
import jax
import jax.numpy as jnp
from jax import lax
from jax.experimental import pallas as pl
from jax.experimental.pallas import tpu as pltpu
from jax.sharding import Mesh, PartitionSpec as P

G = ("zl", "zh", "y")
C = ("x", "core")
Z = ("zl", "zh")
F32 = jnp.float32
BF16 = jnp.bfloat16


def shift(n, s):
    return [(i, (i + s) % n) for i in range(n)]


def z_shift(s):
    at = lambda z: (z % 4) * 2 + z // 4
    return [(at(z), at((z + s) % 8)) for z in range(8)]


def gather_z(t):
    z0 = lax.axis_index("zh") * 4 + lax.axis_index("zl")
    parts = [(0, t)]
    fwd = bwd = t
    for k in range(1, 5):
        fwd = lax.ppermute(fwd, Z, z_shift(1))
        parts.append((-k, fwd))
        if k < 4:
            bwd = lax.ppermute(bwd, Z, z_shift(-1))
            parts.append((k, bwd))
    mine = jnp.zeros((8,) + t.shape, t.dtype)
    for d, part in parts:
        z = (z0 + (d & 7)) & 7
        mine = lax.dynamic_update_slice(mine, part[None], ((z & 3) * 2 + (z >> 2), 0, 0))
    return mine


def ladder_kernel(meta, live, t0, t1, t2, t3, u0, u1, u2, u3, v, wa, wb, keep, away, vm, wm, o2):
    x0, c0, y0, col = meta[0], meta[1], meta[2], meta[3]
    ts, us = (t0, t1, t2, t3), (u0, u1, u2, u3)
    ys = [(y0 + 4 - q) & 3 for q in range(4)]

    @pl.loop(0, 16)
    def _(kt):
        rows = pl.ds(pl.multiple_of(kt * 128, 128), 128)
        for n in range(4):
            tile = v[rows, n * 128 : n * 128 + 128]
            vm[rows, n * 128 : n * 128 + 128] = jnp.where(live[kt, n] != 0, tile, jnp.zeros_like(tile))

    for q in range(4):
        rows = []
        for r in range(8):
            h = (((x0 + r % 4) & 3) << 1) | (c0 ^ (r // 4))
            rows.append(ts[q][h])
        part = jnp.dot(jnp.concatenate(rows, 0), vm[...], preferred_element_type=F32)
        for r in range(8):
            out = (keep, away)[r // 4]
            for a in range(4):
                out[r % 4, pl.ds(ys[q] * 4 + a, 32, stride=16), :] = part[
                    r * 32 : r * 32 + 32, a * 128 : a * 128 + 128
                ]

    lane = lax.broadcasted_iota(jnp.int32, (128, 128), 1)
    acc = jnp.zeros((512, 128), F32)
    for q in range(4):
        w_all = jnp.zeros((128, 128), F32)
        xs = []
        for h in range(8):
            k = h * 4 + ys[q]
            wk = jnp.concatenate([wa[s, k, 0] for s in range(4)] + [wb[s, k, 0] for s in range(4)], 0)
            wk = pltpu.roll(wk.astype(F32), (16 * h + 128 - 16 * col) & 127, 1)
            w_all = jnp.where((lane >> 4) == h, wk, w_all)
            xs.append(jnp.concatenate([wa[s, k, 1] for s in range(4)] + [wb[s, k, 1] for s in range(4)], 0))
        wm[:, q * 128 : q * 128 + 128] = w_all.astype(BF16)
        for h in range(0, 8, 2):
            lhs = jnp.concatenate(
                [us[q][:, (h + e) * 16 : (h + e) * 16 + 16, :].reshape(512, 128) for e in range(2)], 1
            )
            rhs = jnp.concatenate([xs[h], xs[h + 1]], 1)
            acc = acc + lax.dot_general(lhs, rhs, (((1,), (1,)), ((), ())), preferred_element_type=F32)
    o2[...] = acc.T

    own = (lane >> 4) == col

    @pl.loop(0, 16)
    def _(jj):
        j = jj * 2
        rhs = jnp.concatenate(
            [jnp.concatenate([us[q][j + e] for q in range(4)], 0) for e in range(2)], 1
        )
        one = jnp.dot(wm[...], rhs, preferred_element_type=F32)
        two = o2[:, pl.ds(pl.multiple_of((jj >> 2) * 128, 128), 128)]
        for e in range(2):
            placed = pltpu.roll(two, (16 * col + 128 - 16 * ((j + e) & 7)) & 127, 1)
            both = one[:, e * 128 : e * 128 + 128] + jnp.where(own, placed, 0.0)
            rows = pl.ds(pl.multiple_of((j + e) * 16, 16), 16)
            for r in range(8):
                out = (keep, away)[r // 4]
                out[r % 4, rows, :] += both[r * 16 : r * 16 + 16]


def ladder_call(meta, live, ts, us, v, wa, wb):
    smem = pl.BlockSpec(memory_space=pltpu.SMEM)
    vmem = pl.BlockSpec(memory_space=pltpu.VMEM)
    out = jax.ShapeDtypeStruct((4, 512, 128), F32)
    return pl.pallas_call(
        ladder_kernel,
        out_shape=(out, out),
        in_specs=[smem, smem] + [vmem] * 11,
        out_specs=(vmem, vmem),
        scratch_shapes=[
            pltpu.VMEM((2048, 512), BF16),
            pltpu.VMEM((128, 512), BF16),
            pltpu.VMEM((128, 512), F32),
        ],
        cost_estimate=pl.CostEstimate(flops=3_300_000_000, bytes_accessed=15_000_000, transcendentals=0),
        compiler_params=pltpu.CompilerParams(vmem_limit_bytes=48 << 20),
        name="ladder",
    )(meta, live, *ts, *us, v, wa, wb)


def finish_kernel(meta, occ, vir, occ_col, vir_row, p0, p1, p2, p3, p4, out):
    col, g = meta[3], meta[4]
    for il in range(4):
        for a in range(4):
            rows = pl.ds(il * 4 + a, 32, stride=16)
            total = ((p0[rows, :] + p1[rows, :]) + p2[rows, :]) + (p3[rows, :] + p4[rows, :])
            denom = ((vir[g * 4 + a] + vir_row[...]) - occ[col * 4 + il]) - occ_col[...]
            out[il * 32 : il * 32 + 32, a * 128 : a * 128 + 128] = (total / denom).astype(BF16)


def finish_call(meta, eps_occ, eps_vir, parts):
    smem = pl.BlockSpec(memory_space=pltpu.SMEM)
    vmem = pl.BlockSpec(memory_space=pltpu.VMEM)
    return pl.pallas_call(
        finish_kernel,
        out_shape=jax.ShapeDtypeStruct((128, 512), BF16),
        in_specs=[smem] * 3 + [vmem] * 7,
        out_specs=vmem,
        cost_estimate=pl.CostEstimate(flops=400_000, bytes_accessed=1_500_000, transcendentals=0),
        name="finish",
    )(
        meta,
        eps_occ,
        eps_vir,
        jnp.broadcast_to(eps_occ[:, None], (32, 128)),
        eps_vir[None, :],
        *parts,
    )


def local(amplitudes, ladder_ints, tile_live, cycle_direct, cycle_exchange, eps_occ, eps_vir):
    x0, c0, y0 = lax.axis_index("x"), lax.axis_index("core"), lax.axis_index("y")
    meta = jnp.stack([x0, c0, y0, lax.axis_index(C), lax.axis_index(G)]).astype(jnp.int32)
    mine = gather_z(amplitudes)
    both = jnp.stack([cycle_direct, cycle_exchange]).reshape(2, 4, 32, 4, 128)
    both = both.transpose(2, 0, 1, 3, 4).reshape(32, 2, 16, 128)
    both = lax.all_to_all(both, G, 0, 0, tiled=True)
    wa = jnp.stack([both] + [lax.ppermute(both, "x", shift(4, -s)) for s in (1, 2, 3)])
    wb = lax.ppermute(wa, "core", shift(2, 1))
    ts = [mine] + [lax.ppermute(mine, "y", shift(4, s)) for s in (1, 2, 3)]
    us = [t.reshape(8, 32, 16, 128).transpose(1, 0, 2, 3).reshape(32, 128, 128) for t in ts]
    keep, away = ladder_call(meta, tile_live, ts, us, ladder_ints, wa, wb)
    got = lax.ppermute(away, "core", shift(2, 1))
    parts = [keep[0], got[0]]
    for s in (1, 2, 3):
        parts.append(lax.ppermute(keep[s] + got[s], "x", shift(4, s)))
    return finish_call(meta, eps_occ, eps_vir, parts)


def solution(mesh):
    fine = Mesh(mesh.devices.reshape(4, 2, 4, 4, 2), ("zl", "zh", "y", "x", "core"))
    placed = (P(G, C), P(C, G), P(C, G), P(C, G), P(C, G), P(), P())
    return jax.shard_map(local, mesh=fine, in_specs=placed, out_specs=P(C, G), check_vma=False)
```

```python
import jax
import jax.numpy as jnp
from jax import lax
from jax.experimental import pallas as pl
from jax.experimental.pallas import tpu as pltpu
from jax.sharding import Mesh, PartitionSpec as P

G = ("zl", "zh", "y")
C = ("x", "core")
Z = ("zl", "zh")
J = 16
F32 = jnp.float32
BF16 = jnp.bfloat16


def shift(n, s):
    return [(i, (i + s) % n) for i in range(n)]


def z_shift(s):
    at = lambda z: (z % 4) * 2 + z // 4
    return [(at(z), at((z + s) % 8)) for z in range(8)]


def ladder_kernel(meta, live, t0, t1, t2, t3, u0, u1, u2, u3, v, wa, wb, keep, away, vm, wm, o2):
    x0, c0, y0, col = meta[0], meta[1], meta[2], meta[3]
    ts, us = (t0, t1, t2, t3), (u0, u1, u2, u3)
    ys = [(y0 + 4 - q) & 3 for q in range(4)]

    @pl.loop(0, 16)
    def _(kt):
        rows = pl.ds(pl.multiple_of(kt * 128, 128), 128)
        for n in range(4):
            tile = v[rows, n * 128 : n * 128 + 128]
            vm[rows, n * 128 : n * 128 + 128] = jnp.where(live[kt, n] != 0, tile, jnp.zeros_like(tile))

    for q in range(0, 4, 2):
        rows = []
        for e in range(2):
            for r in range(8):
                h = (((x0 + r % 4) & 3) << 1) | (c0 ^ (r // 4))
                rows.append(ts[q + e][h])
        part = jnp.dot(jnp.concatenate(rows, 0), vm[...], preferred_element_type=F32)
        for e in range(2):
            for r in range(8):
                out = (keep, away)[r // 4]
                at = (e * 8 + r) * J
                for a in range(4):
                    out[r % 4, pl.ds(ys[q + e] * 4 + a, J, stride=16), :] = part[
                        at : at + J, a * 128 : a * 128 + 128
                    ]

    lane = lax.broadcasted_iota(jnp.int32, (128, 128), 1)
    acc = jnp.zeros((J * 16, 128), F32)
    for q in range(4):
        w_all = jnp.zeros((128, 128), F32)
        xs = []
        for h in range(8):
            k = h * 4 + ys[q]
            wk = jnp.concatenate([wa[s, k, 0] for s in range(4)] + [wb[s, k, 0] for s in range(4)], 0)
            wk = pltpu.roll(wk.astype(F32), (16 * h + 128 - 16 * col) & 127, 1)
            w_all = jnp.where((lane >> 4) == h, wk, w_all)
            xs.append(jnp.concatenate([wa[s, k, 1] for s in range(4)] + [wb[s, k, 1] for s in range(4)], 0))
        wm[:, q * 128 : q * 128 + 128] = w_all.astype(BF16)
        for h in range(0, 8, 2):
            lhs = jnp.concatenate(
                [us[q][:, (h + e) * 16 : (h + e) * 16 + 16, :].reshape(J * 16, 128) for e in range(2)], 1
            )
            rhs = jnp.concatenate([xs[h], xs[h + 1]], 1)
            acc = acc + lax.dot_general(lhs, rhs, (((1,), (1,)), ((), ())), preferred_element_type=F32)
    o2[...] = acc.T

    own = (lane >> 4) == col

    @pl.loop(0, J // 2)
    def _(jj):
        j = jj * 2
        rhs = jnp.concatenate(
            [jnp.concatenate([us[q][j + e] for q in range(4)], 0) for e in range(2)], 1
        )
        one = jnp.dot(wm[...], rhs, preferred_element_type=F32)
        two = o2[:, pl.ds(pl.multiple_of((jj >> 2) * 128, 128), 128)]
        for e in range(2):
            placed = pltpu.roll(two, (16 * col + 128 - 16 * ((j + e) & 7)) & 127, 1)
            both = one[:, e * 128 : e * 128 + 128] + jnp.where(own, placed, 0.0)
            rows = pl.ds(pl.multiple_of((j + e) * 16, 16), 16)
            for r in range(8):
                out = (keep, away)[r // 4]
                out[r % 4, rows, :] += both[r * 16 : r * 16 + 16]


def ladder_call(meta, live, ts, us, v, wa, wb):
    smem = pl.BlockSpec(memory_space=pltpu.SMEM)
    vmem = pl.BlockSpec(memory_space=pltpu.VMEM)
    out = jax.ShapeDtypeStruct((4, J * 16, 128), F32)
    return pl.pallas_call(
        ladder_kernel,
        out_shape=(out, out),
        in_specs=[smem, smem] + [vmem] * 11,
        out_specs=(vmem, vmem),
        scratch_shapes=[
            pltpu.VMEM((2048, 512), BF16),
            pltpu.VMEM((128, 512), BF16),
            pltpu.VMEM((128, J * 16), F32),
        ],
        cost_estimate=pl.CostEstimate(flops=1_650_000_000, bytes_accessed=10_000_000, transcendentals=0),
        compiler_params=pltpu.CompilerParams(vmem_limit_bytes=24 << 20),
        name="ladder",
    )(meta, live, *ts, *us, v, wa, wb)


def finish_kernel(meta, occ, vir, occ_col, vir_row, *refs):
    col, g = meta[3], meta[4]
    out = refs[-1]
    for half in range(32 // J):
        p0, p1, p2, p3, p4 = refs[half * 5 : half * 5 + 5]
        for il in range(4):
            for a in range(4):
                rows = pl.ds(il * 4 + a, J, stride=16)
                total = ((p0[rows, :] + p1[rows, :]) + p2[rows, :]) + (p3[rows, :] + p4[rows, :])
                denom = ((vir[g * 4 + a] + vir_row[...]) - occ[col * 4 + il]) - occ_col[
                    half * J : half * J + J, :
                ]
                at = il * 32 + half * J
                out[at : at + J, a * 128 : a * 128 + 128] = (total / denom).astype(BF16)


def finish_call(meta, eps_occ, eps_vir, parts):
    smem = pl.BlockSpec(memory_space=pltpu.SMEM)
    vmem = pl.BlockSpec(memory_space=pltpu.VMEM)
    return pl.pallas_call(
        finish_kernel,
        out_shape=jax.ShapeDtypeStruct((128, 512), BF16),
        in_specs=[smem] * 3 + [vmem] * (2 + len(parts)),
        out_specs=vmem,
        cost_estimate=pl.CostEstimate(flops=400_000, bytes_accessed=1_500_000, transcendentals=0),
        name="finish",
    )(
        meta,
        eps_occ,
        eps_vir,
        jnp.broadcast_to(eps_occ[:, None], (32, 128)),
        eps_vir[None, :],
        *parts,
    )


def local(amplitudes, ladder_ints, tile_live, cycle_direct, cycle_exchange, eps_occ, eps_vir):
    x0, c0, y0 = lax.axis_index("x"), lax.axis_index("core"), lax.axis_index("y")
    meta = jnp.stack([x0, c0, y0, lax.axis_index(C), lax.axis_index(G)]).astype(jnp.int32)
    copies = [jnp.broadcast_to(amplitudes[n * J : n * J + J], (8, J, 2048)) for n in range(32 // J)]
    both = jnp.stack([cycle_direct, cycle_exchange]).reshape(2, 4, 32, 4, 128)
    both = both.transpose(2, 0, 1, 3, 4).reshape(32, 2, 16, 128)
    both = lax.all_to_all(both, G, 0, 0, tiled=True)
    xs = [both] + [lax.ppermute(both, "x", shift(4, -s)) for s in (1, 2, 3)]
    mines = [lax.all_to_all(c, Z, 0, 0, tiled=True) for c in copies]
    tss = [[mine] + [lax.ppermute(mine, "y", shift(4, s)) for s in (1, 2, 3)] for mine in mines]
    *xs, tss[0][1] = lax.optimization_barrier((*xs, tss[0][1]))
    wa = jnp.stack(xs)
    wb = lax.ppermute(wa, "core", shift(2, 1))
    parts = []
    for ts in tss:
        us = [t.reshape(8, J, 16, 128).transpose(1, 0, 2, 3).reshape(J, 128, 128) for t in ts]
        keep, away = ladder_call(meta, tile_live, ts, us, ladder_ints, wa, wb)
        away, *parts = lax.optimization_barrier((away, *parts))
        got = lax.ppermute(away, "core", shift(2, 1))
        sums = [keep[s] + got[s] for s in (1, 2, 3)]
        *sums, wa = lax.optimization_barrier((*sums, wa))
        parts += [keep[0], got[0]]
        parts += [lax.ppermute(block, "x", shift(4, s)) for s, block in zip((1, 2, 3), sums)]
    return finish_call(meta, eps_occ, eps_vir, parts)


def solution(mesh):
    fine = Mesh(mesh.devices.reshape(4, 2, 4, 4, 2), ("zl", "zh", "y", "x", "core"))
    placed = (P(G, C), P(C, G), P(C, G), P(C, G), P(C, G), P(), P())
    return jax.shard_map(local, mesh=fine, in_specs=placed, out_specs=P(C, G), check_vma=False)
```

```python
import functools

import jax
import jax.numpy as jnp
from jax import lax
from jax.experimental import pallas as pl
from jax.experimental.pallas import tpu as pltpu
from jax.sharding import Mesh, PartitionSpec as P

G = ("zl", "zh", "y")
C = ("x", "core")
Z = ("zl", "zh")
F32 = jnp.float32
BF16 = jnp.bfloat16


def shift(n, s):
    return [(i, (i + s) % n) for i in range(n)]


def z_shift(s):
    at = lambda z: (z % 4) * 2 + z // 4
    return [(at(z), at((z + s) % 8)) for z in range(8)]


EVEN = (6, 0, 2, 4)
ODD = (5, 7, 1, 3)


def ladder_kernel(slots, meta, live, *refs):
    ts, us, (v, wa, wb), refs = refs[:4], refs[4:8], refs[8:11], refs[11:]
    prev = None
    if slots is ODD:
        prev, refs = refs[0], refs[1:]
    outs, (ladder, vm, wm, o2) = refs[:-4], refs[-4:]
    x0, c0, y0, col, z0 = meta[0], meta[1], meta[2], meta[3], meta[5]
    ys = [(y0 + 4 - q) & 3 for q in range(4)]
    zs = [(z0 + d) & 7 for d in slots]
    hs = [((z & 3) << 1) | (z >> 2) for z in zs]
    at = [((((z >> 2) ^ c0) << 2) | (((z & 3) + 4 - x0) & 3)) for z in zs]

    @pl.loop(0, 16)
    def _(kt):
        rows = pl.ds(pl.multiple_of(kt * 128, 128), 128)
        for n in range(4):
            tile = v[rows, n * 128 : n * 128 + 128]
            vm[rows, n * 128 : n * 128 + 128] = jnp.where(live[kt, n] != 0, tile, jnp.zeros_like(tile))

    @pl.loop(0, 8)
    def _(r):
        ladder[r] = jnp.zeros((512, 128), F32) if prev is None else prev[r]

    for q in range(0, 4, 2):
        rows = jnp.concatenate([ts[q][...].reshape(128, 2048), ts[q + 1][...].reshape(128, 2048)], 0)
        part = jnp.dot(rows, vm[...], preferred_element_type=F32)
        for e in range(2):
            for d in range(4):
                top = e * 128 + d * 32
                for a in range(4):
                    rows = pl.ds(ys[q + e] * 4 + a, 32, stride=16)
                    ladder[at[d], rows, :] += part[top : top + 32, a * 128 : a * 128 + 128]

    lane = lax.broadcasted_iota(jnp.int32, (128, 128), 1)

    def spread(k, which):
        pieces = [w[(x0 + s) & 3, k, which] for w in (wa, wb) for s in range(4)]
        return jnp.concatenate(pieces, 0)

    acc = jnp.zeros((512, 128), F32)
    for p in range(2):
        w_all = jnp.zeros((128, 128), F32)
        for e in range(2):
            q = p * 2 + e
            ks = [h * 4 + ys[q] for h in hs]
            for d in range(4):
                wk = spread(ks[d], 0).astype(F32)
                wk = pltpu.roll(wk, (16 * (e * 4 + d) + 128 - 16 * col) & 127, 1)
                w_all = jnp.where((lane >> 4) == e * 4 + d, wk, w_all)
            for d in range(0, 4, 2):
                lhs = jnp.concatenate([us[q][d + f].reshape(512, 128) for f in range(2)], 1)
                rhs = jnp.concatenate([spread(ks[d + f], 1) for f in range(2)], 1)
                acc = acc + lax.dot_general(lhs, rhs, (((1,), (1,)), ((), ())), preferred_element_type=F32)
        wm[:, p * 128 : p * 128 + 128] = w_all.astype(BF16)
    o2[...] = acc.T

    own = (lane >> 4) == col

    @pl.loop(0, 16)
    def _(jj):
        j = jj * 2
        rhs = jnp.concatenate(
            [jnp.concatenate([us[q][d, j + e] for q in range(4) for d in range(4)], 0) for e in range(2)], 1
        )
        one = jnp.dot(wm[...], rhs, preferred_element_type=F32)
        two = o2[:, pl.ds(pl.multiple_of((jj >> 2) * 128, 128), 128)]
        for e in range(2):
            placed = pltpu.roll(two, (16 * col + 128 - 16 * ((j + e) & 7)) & 127, 1)
            both = one[:, e * 128 : e * 128 + 128] + jnp.where(own, placed, 0.0)
            rows = pl.ds(pl.multiple_of((j + e) * 16, 16), 16)
            for r in range(8):
                value = ladder[r, rows, :] + both[r * 16 : r * 16 + 16]
                if prev is None:
                    outs[0][r, rows, :] = value
                else:
                    outs[r // 4][r % 4, rows, :] = value


def ladder_call(slots, meta, live, ts, us, v, wa, wb, prev=()):
    smem = pl.BlockSpec(memory_space=pltpu.SMEM)
    vmem = pl.BlockSpec(memory_space=pltpu.VMEM)
    whole = jax.ShapeDtypeStruct((8, 512, 128), F32)
    half = jax.ShapeDtypeStruct((4, 512, 128), F32)
    return pl.pallas_call(
        functools.partial(ladder_kernel, slots),
        out_shape=(half, half) if prev else (whole,),
        in_specs=[smem, smem] + [vmem] * (11 + len(prev)),
        out_specs=(vmem, vmem) if prev else (vmem,),
        scratch_shapes=[
            pltpu.VMEM((8, 512, 128), F32),
            pltpu.VMEM((2048, 512), BF16),
            pltpu.VMEM((128, 256), BF16),
            pltpu.VMEM((128, 512), F32),
        ],
        cost_estimate=pl.CostEstimate(flops=1_650_000_000, bytes_accessed=10_000_000, transcendentals=0),
        compiler_params=pltpu.CompilerParams(vmem_limit_bytes=24 << 20),
        name="ladder",
    )(meta, live, *ts, *us, v, wa, wb, *prev)


def finish_kernel(meta, occ, vir, occ_col, vir_row, p0, p1, p2, p3, p4, out):
    col, g = meta[3], meta[4]
    for il in range(4):
        for a in range(4):
            rows = pl.ds(il * 4 + a, 32, stride=16)
            total = ((p0[rows, :] + p1[rows, :]) + p2[rows, :]) + (p3[rows, :] + p4[rows, :])
            denom = ((vir[g * 4 + a] + vir_row[...]) - occ[col * 4 + il]) - occ_col[...]
            out[il * 32 : il * 32 + 32, a * 128 : a * 128 + 128] = (total / denom).astype(BF16)


def finish_call(meta, eps_occ, eps_vir, parts):
    smem = pl.BlockSpec(memory_space=pltpu.SMEM)
    vmem = pl.BlockSpec(memory_space=pltpu.VMEM)
    return pl.pallas_call(
        finish_kernel,
        out_shape=jax.ShapeDtypeStruct((128, 512), BF16),
        in_specs=[smem] * 3 + [vmem] * 7,
        out_specs=vmem,
        cost_estimate=pl.CostEstimate(flops=400_000, bytes_accessed=1_500_000, transcendentals=0),
        name="finish",
    )(
        meta,
        eps_occ,
        eps_vir,
        jnp.broadcast_to(eps_occ[:, None], (32, 128)),
        eps_vir[None, :],
        *parts,
    )


def over_y(group):
    return [group] + [lax.ppermute(group, "y", shift(4, s)) for s in (1, 2, 3)]


def split_rows(ts):
    return [t.reshape(4, 32, 16, 128) for t in ts]


def local(amplitudes, ladder_ints, tile_live, cycle_direct, cycle_exchange, eps_occ, eps_vir):
    x0, c0, y0 = lax.axis_index("x"), lax.axis_index("core"), lax.axis_index("y")
    z0 = lax.axis_index("zh") * 4 + lax.axis_index("zl")
    meta = jnp.stack([x0, c0, y0, lax.axis_index(C), lax.axis_index(G), z0]).astype(jnp.int32)
    t = amplitudes
    below, above, across = (lax.ppermute(t, Z, z_shift(s)) for s in (2, -2, 4))
    both = jnp.stack([cycle_direct, cycle_exchange]).reshape(2, 4, 32, 4, 128)
    both = both.transpose(2, 0, 1, 3, 4).reshape(32, 2, 16, 128)
    both = lax.all_to_all(both, G, 0, 0, tiled=True)
    both, below, above, across = lax.optimization_barrier((both, below, above, across))
    even = jnp.stack([below, t, above, across])
    left = lax.ppermute(even[0:2], Z, z_shift(1))
    right = lax.ppermute(even[1:3], Z, z_shift(-1))
    ts_even = over_y(even)
    wa = lax.all_to_all(jnp.broadcast_to(both[None], (4, 32, 2, 16, 128)), "x", 0, 0, tiled=True)
    wa, left, right, ts_even[1] = lax.optimization_barrier((wa, left, right, ts_even[1]))
    wb = lax.ppermute(wa, "core", shift(2, 1))
    odd = jnp.concatenate([left, right])
    ts_odd = over_y(odd)
    prev = list(ladder_call(EVEN, meta, tile_live, ts_even, split_rows(ts_even), ladder_ints, wa, wb))
    *ts_odd, prev[0] = lax.optimization_barrier((*ts_odd, prev[0]))
    keep, away = ladder_call(ODD, meta, tile_live, ts_odd, split_rows(ts_odd), ladder_ints, wa, wb, tuple(prev))
    got = lax.ppermute(away, "core", shift(2, 1))
    parts = [keep[0], got[0]]
    for s in (1, 2, 3):
        parts.append(lax.ppermute(keep[s] + got[s], "x", shift(4, s)))
    return finish_call(meta, eps_occ, eps_vir, parts)


def solution(mesh):
    fine = Mesh(mesh.devices.reshape(4, 2, 4, 4, 2), ("zl", "zh", "y", "x", "core"))
    placed = (P(G, C), P(C, G), P(C, G), P(C, G), P(C, G), P(), P())
    return jax.shard_map(local, mesh=fine, in_specs=placed, out_specs=P(C, G), check_vma=False)
```

```python
import functools

import jax
import jax.numpy as jnp
from jax import lax
from jax.experimental import pallas as pl
from jax.experimental.pallas import tpu as pltpu
from jax.sharding import Mesh, PartitionSpec as P

G = ("zl", "zh", "y")
C = ("x", "core")
Z = ("zl", "zh")
F32 = jnp.float32
BF16 = jnp.bfloat16


def shift(n, s):
    return [(i, (i + s) % n) for i in range(n)]


def z_shift(s):
    at = lambda z: (z % 4) * 2 + z // 4
    return [(at(z), at((z + s) % 8)) for z in range(8)]


NEAR = (0, -1, 1, -2, 2)
FAR = (-3, 3, 4)
CUTS = {NEAR: 3, FAR: 1}


def ladder_kernel(slots, meta, live, *refs):
    n = len(slots)
    cut = CUTS[slots]
    ts, us, (v, wa, wb), refs = refs[:5], refs[5:10], refs[10:13], refs[13:]
    blocks = [(p, d, q, d) for p, q in ((0, 0), (1, 1)) for d in range(n)]
    blocks += [(2, d, 2, d) for d in range(cut)] + [(3, d - cut, 2, d) for d in range(cut, n)]
    blocks += [(4, d, 3, d) for d in range(n)]
    prev = None
    if slots is FAR:
        prev, refs = refs[0], refs[1:]
    outs, (ladder, vm, wm, o2) = refs[:-4], refs[-4:]
    x0, c0, y0, col, z0 = meta[0], meta[1], meta[2], meta[3], meta[5]
    ys = [(y0 + 4 - q) & 3 for q in range(4)]
    zs = [(z0 + (d & 7)) & 7 for d in slots]
    hs = [((z & 3) << 1) | (z >> 2) for z in zs]
    at = [((((z >> 2) ^ c0) << 2) | (((z & 3) + 4 - x0) & 3)) for z in zs]

    @pl.loop(0, 16)
    def _(kt):
        rows = pl.ds(pl.multiple_of(kt * 128, 128), 128)
        for n in range(4):
            tile = v[rows, n * 128 : n * 128 + 128]
            vm[rows, n * 128 : n * 128 + 128] = jnp.where(live[kt, n] != 0, tile, jnp.zeros_like(tile))

    @pl.loop(0, 8)
    def _(r):
        ladder[r] = jnp.zeros((512, 128), F32) if prev is None else prev[r]

    half = 2 * n
    for part_of in (blocks[:half], blocks[half:]):
        rows = jnp.concatenate([ts[p][e] for p, e, _, _ in part_of], 0)
        part = jnp.dot(rows, vm[...], preferred_element_type=F32)
        for m, (_, _, q, d) in enumerate(part_of):
            for a in range(4):
                rows = pl.ds(ys[q] * 4 + a, 32, stride=16)
                ladder[at[d], rows, :] += part[m * 32 : m * 32 + 32, a * 128 : a * 128 + 128]

    lane = lax.broadcasted_iota(jnp.int32, (128, 128), 1)

    def spread(k, which):
        pieces = [w[(x0 + s) & 3, k, which] for w in (wa, wb) for s in range(4)]
        return jnp.concatenate(pieces, 0)

    acc = jnp.zeros((512, 128), F32)
    w_all = None
    for m in range(0, 4 * n, 2):
        pair = blocks[m : m + 2]
        lhs = jnp.concatenate([us[p][e].reshape(512, 128) for p, e, _, _ in pair], 1)
        rhs = jnp.concatenate([spread(hs[d] * 4 + ys[q], 1) for _, _, q, d in pair], 1)
        acc = acc + lax.dot_general(lhs, rhs, (((1,), (1,)), ((), ())), preferred_element_type=F32)
        if m % 8 == 0:
            w_all = jnp.zeros((128, 128), F32)
        for f, (_, _, q, d) in enumerate(pair):
            place = m % 8 + f
            wk = spread(hs[d] * 4 + ys[q], 0).astype(F32)
            wk = pltpu.roll(wk, (16 * place + 128 - 16 * col) & 127, 1)
            w_all = jnp.where((lane >> 4) == place, wk, w_all)
        if m % 8 == 6 or m + 2 == 4 * n:
            top = m // 8 * 128
            width = min(128, 64 * n - top)
            wm[:, top : top + width] = w_all[:, :width].astype(BF16)
    o2[...] = acc.T

    own = (lane >> 4) == col

    @pl.loop(0, 16)
    def _(jj):
        j = jj * 2
        rhs = jnp.concatenate(
            [jnp.concatenate([us[p][e, j + f] for p, e, _, _ in blocks], 0) for f in range(2)], 1
        )
        one = jnp.dot(wm[...], rhs, preferred_element_type=F32)
        two = o2[:, pl.ds(pl.multiple_of((jj >> 2) * 128, 128), 128)]
        for f in range(2):
            placed = pltpu.roll(two, (16 * col + 128 - 16 * ((j + f) & 7)) & 127, 1)
            both = one[:, f * 128 : f * 128 + 128] + jnp.where(own, placed, 0.0)
            rows = pl.ds(pl.multiple_of((j + f) * 16, 16), 16)
            for r in range(8):
                value = ladder[r, rows, :] + both[r * 16 : r * 16 + 16]
                if prev is None:
                    outs[0][r, rows, :] = value
                else:
                    outs[r // 4][r % 4, rows, :] = value


def ladder_call(slots, meta, live, ts, us, v, wa, wb, prev=()):
    smem = pl.BlockSpec(memory_space=pltpu.SMEM)
    vmem = pl.BlockSpec(memory_space=pltpu.VMEM)
    whole = jax.ShapeDtypeStruct((8, 512, 128), F32)
    half = jax.ShapeDtypeStruct((4, 512, 128), F32)
    return pl.pallas_call(
        functools.partial(ladder_kernel, slots),
        out_shape=(half, half) if prev else (whole,),
        in_specs=[smem, smem] + [vmem] * (13 + len(prev)),
        out_specs=(vmem, vmem) if prev else (vmem,),
        scratch_shapes=[
            pltpu.VMEM((8, 512, 128), F32),
            pltpu.VMEM((2048, 512), BF16),
            pltpu.VMEM((128, 64 * len(slots)), BF16),
            pltpu.VMEM((128, 512), F32),
        ],
        cost_estimate=pl.CostEstimate(flops=400_000_000 * len(slots), bytes_accessed=10_000_000, transcendentals=0),
        compiler_params=pltpu.CompilerParams(vmem_limit_bytes=24 << 20),
        name="ladder",
    )(meta, live, *ts, *us, v, wa, wb, *prev)


def finish_kernel(meta, occ, vir, occ_col, vir_row, p0, p1, p2, p3, p4, out):
    col, g = meta[3], meta[4]
    for il in range(4):
        for a in range(4):
            rows = pl.ds(il * 4 + a, 32, stride=16)
            total = ((p0[rows, :] + p1[rows, :]) + p2[rows, :]) + (p3[rows, :] + p4[rows, :])
            denom = ((vir[g * 4 + a] + vir_row[...]) - occ[col * 4 + il]) - occ_col[...]
            out[il * 32 : il * 32 + 32, a * 128 : a * 128 + 128] = (total / denom).astype(BF16)


def finish_call(meta, eps_occ, eps_vir, parts):
    smem = pl.BlockSpec(memory_space=pltpu.SMEM)
    vmem = pl.BlockSpec(memory_space=pltpu.VMEM)
    return pl.pallas_call(
        finish_kernel,
        out_shape=jax.ShapeDtypeStruct((128, 512), BF16),
        in_specs=[smem] * 3 + [vmem] * 7,
        out_specs=vmem,
        cost_estimate=pl.CostEstimate(flops=400_000, bytes_accessed=1_500_000, transcendentals=0),
        name="finish",
    )(
        meta,
        eps_occ,
        eps_vir,
        jnp.broadcast_to(eps_occ[:, None], (32, 128)),
        eps_vir[None, :],
        *parts,
    )


def over_y(group, cut):
    down = lax.ppermute(group, "y", shift(4, 1))
    up = lax.ppermute(group, "y", shift(4, -1))
    first = lax.ppermute(down[:cut], "y", shift(4, 1))
    rest = lax.ppermute(up[cut:], "y", shift(4, -1))
    return [group, down, first, rest, up]


def split_rows(ts):
    return [t.reshape(-1, 32, 16, 128) for t in ts]


def local(amplitudes, ladder_ints, tile_live, cycle_direct, cycle_exchange, eps_occ, eps_vir):
    x0, c0, y0 = lax.axis_index("x"), lax.axis_index("core"), lax.axis_index("y")
    z0 = lax.axis_index("zh") * 4 + lax.axis_index("zl")
    meta = jnp.stack([x0, c0, y0, lax.axis_index(C), lax.axis_index(G), z0]).astype(jnp.int32)
    both = jnp.stack([cycle_direct, cycle_exchange]).reshape(2, 4, 32, 4, 128)
    both = both.transpose(2, 0, 1, 3, 4).reshape(32, 2, 16, 128)
    fwd = bwd = amplitudes
    ring = [amplitudes]
    for k in range(1, 4):
        fwd, bwd = lax.ppermute(fwd, Z, z_shift(1)), lax.ppermute(bwd, Z, z_shift(-1))
        ring += [fwd, bwd]
    ring.append(lax.ppermute(fwd, Z, z_shift(1)))
    near = jnp.stack(ring[:5])
    both = lax.all_to_all(both, G, 0, 0, tiled=True)
    wa = lax.all_to_all(jnp.broadcast_to(both[None], (4, 32, 2, 16, 128)), "x", 0, 0, tiled=True)
    wa, ring[7] = lax.optimization_barrier((wa, ring[7]))
    wb = lax.ppermute(wa, "core", shift(2, 1))
    far = jnp.stack(ring[5:])
    ts_near, ts_far = over_y(near, CUTS[NEAR]), over_y(far, CUTS[FAR])
    prev = list(ladder_call(NEAR, meta, tile_live, ts_near, split_rows(ts_near), ladder_ints, wa, wb))
    *ts_far, prev[0] = lax.optimization_barrier((*ts_far, prev[0]))
    keep, away = ladder_call(FAR, meta, tile_live, ts_far, split_rows(ts_far), ladder_ints, wa, wb, tuple(prev))
    got = lax.ppermute(away, "core", shift(2, 1))
    parts = [keep[0], got[0]]
    for s in (1, 2, 3):
        parts.append(lax.ppermute(keep[s] + got[s], "x", shift(4, s)))
    return finish_call(meta, eps_occ, eps_vir, parts)


def solution(mesh):
    fine = Mesh(mesh.devices.reshape(4, 2, 4, 4, 2), ("zl", "zh", "y", "x", "core"))
    placed = (P(G, C), P(C, G), P(C, G), P(C, G), P(C, G), P(), P())
    return jax.shard_map(local, mesh=fine, in_specs=placed, out_specs=P(C, G), check_vma=False)
```

```python
import functools

import jax
import jax.numpy as jnp
from jax import lax
from jax.experimental import pallas as pl
from jax.experimental.pallas import tpu as pltpu
from jax.sharding import Mesh, PartitionSpec as P

G = ("zl", "zh", "y")
C = ("x", "core")
Z = ("zl", "zh")
F32 = jnp.float32
BF16 = jnp.bfloat16


def shift(n, s):
    return [(i, (i + s) % n) for i in range(n)]


def z_shift(s):
    at = lambda z: (z % 4) * 2 + z // 4
    return [(at(z), at((z + s) % 8)) for z in range(8)]


FIRST = ((0, 0, 8), (1, 0, 8), (3, 0, 8))
LAST = ((2, 0, 4), (2, 4, 4))


def ladder_kernel(pieces, meta, live, *refs):
    n = len(pieces)
    ts, us, (v, wa, wb), refs = refs[:n], refs[n : 2 * n], refs[2 * n : 2 * n + 3], refs[2 * n + 3 :]
    blocks = [(p, e, q, top + e) for p, (q, top, count) in enumerate(pieces) for e in range(count)]
    prev = None
    if pieces is LAST:
        prev, refs = refs[0], refs[1:]
    outs, (ladder, vm, wm, o2) = refs[:-4], refs[-4:]
    x0, c0, y0, col = meta[0], meta[1], meta[2], meta[3]
    ys = [(y0 + 4 - q) & 3 for q in range(4)]
    at = [(((h & 1) ^ c0) << 2) | (((h >> 1) + 4 - x0) & 3) for h in range(8)]

    @pl.loop(0, 16)
    def _(kt):
        rows = pl.ds(pl.multiple_of(kt * 128, 128), 128)
        for n in range(4):
            tile = v[rows, n * 128 : n * 128 + 128]
            vm[rows, n * 128 : n * 128 + 128] = jnp.where(live[kt, n] != 0, tile, jnp.zeros_like(tile))

    @pl.loop(0, 8)
    def _(r):
        ladder[r] = jnp.zeros((512, 128), F32) if prev is None else prev[r]

    for m0 in range(0, len(blocks), 8):
        part_of = blocks[m0 : m0 + 8]
        rows = jnp.concatenate([ts[p][e] for p, e, _, _ in part_of], 0)
        part = jnp.dot(rows, vm[...], preferred_element_type=F32)
        for m, (_, _, q, h) in enumerate(part_of):
            for a in range(4):
                rows = pl.ds(ys[q] * 4 + a, 32, stride=16)
                ladder[at[h], rows, :] += part[m * 32 : m * 32 + 32, a * 128 : a * 128 + 128]

    lane = lax.broadcasted_iota(jnp.int32, (128, 128), 1)

    def spread(k, which):
        pieces = [w[s, k, which] for w in (wa, wb) for s in range(4)]
        return jnp.concatenate(pieces, 0)

    acc = jnp.zeros((512, 128), F32)
    w_all = None
    for m in range(0, len(blocks), 2):
        pair = blocks[m : m + 2]
        lhs = jnp.concatenate([us[p][e].reshape(512, 128) for p, e, _, _ in pair], 1)
        rhs = jnp.concatenate([spread(h * 4 + ys[q], 1) for _, _, q, h in pair], 1)
        acc = acc + lax.dot_general(lhs, rhs, (((1,), (1,)), ((), ())), preferred_element_type=F32)
        if m % 8 == 0:
            w_all = jnp.zeros((128, 128), F32)
        for f, (_, _, q, h) in enumerate(pair):
            place = m % 8 + f
            wk = spread(h * 4 + ys[q], 0).astype(F32)
            wk = pltpu.roll(wk, (16 * place + 128 - 16 * col) & 127, 1)
            w_all = jnp.where((lane >> 4) == place, wk, w_all)
        if m % 8 == 6:
            wm[:, m // 8 * 128 : m // 8 * 128 + 128] = w_all.astype(BF16)
    o2[...] = acc.T

    own = (lane >> 4) == col

    @pl.loop(0, 16)
    def _(jj):
        j = jj * 2
        rhs = jnp.concatenate(
            [jnp.concatenate([us[p][e, j + f] for p, e, _, _ in blocks], 0) for f in range(2)], 1
        )
        one = jnp.dot(wm[...], rhs, preferred_element_type=F32)
        two = o2[:, pl.ds(pl.multiple_of((jj >> 2) * 128, 128), 128)]
        for f in range(2):
            placed = pltpu.roll(two, (16 * col + 128 - 16 * ((j + f) & 7)) & 127, 1)
            both = one[:, f * 128 : f * 128 + 128] + jnp.where(own, placed, 0.0)
            rows = pl.ds(pl.multiple_of((j + f) * 16, 16), 16)
            for r in range(8):
                value = ladder[r, rows, :] + both[r * 16 : r * 16 + 16]
                if prev is None:
                    outs[0][r, rows, :] = value
                else:
                    outs[r // 4][r % 4, rows, :] = value


def ladder_call(pieces, meta, live, ts, us, v, wa, wb, prev=()):
    smem = pl.BlockSpec(memory_space=pltpu.SMEM)
    vmem = pl.BlockSpec(memory_space=pltpu.VMEM)
    whole = jax.ShapeDtypeStruct((8, 512, 128), F32)
    half = jax.ShapeDtypeStruct((4, 512, 128), F32)
    return pl.pallas_call(
        functools.partial(ladder_kernel, pieces),
        out_shape=(half, half) if prev else (whole,),
        in_specs=[smem, smem] + [vmem] * (len(ts) + len(us) + 3 + len(prev)),
        out_specs=(vmem, vmem) if prev else (vmem,),
        scratch_shapes=[
            pltpu.VMEM((8, 512, 128), F32),
            pltpu.VMEM((2048, 512), BF16),
            pltpu.VMEM((128, 384 if prev == () else 128), BF16),
            pltpu.VMEM((128, 512), F32),
        ],
        cost_estimate=pl.CostEstimate(flops=400_000_000 * (9 if prev == () else 3), bytes_accessed=10_000_000, transcendentals=0),
        compiler_params=pltpu.CompilerParams(vmem_limit_bytes=24 << 20),
        name="ladder",
    )(meta, live, *ts, *us, v, wa, wb, *prev)


def finish_kernel(meta, occ, vir, occ_col, vir_row, p0, p1, p2, p3, p4, out):
    col, g = meta[3], meta[4]
    for il in range(4):
        for a in range(4):
            rows = pl.ds(il * 4 + a, 32, stride=16)
            total = ((p0[rows, :] + p1[rows, :]) + p2[rows, :]) + (p3[rows, :] + p4[rows, :])
            denom = ((vir[g * 4 + a] + vir_row[...]) - occ[col * 4 + il]) - occ_col[...]
            out[il * 32 : il * 32 + 32, a * 128 : a * 128 + 128] = (total / denom).astype(BF16)


def finish_call(meta, occ_col, eps_occ, eps_vir, parts):
    smem = pl.BlockSpec(memory_space=pltpu.SMEM)
    vmem = pl.BlockSpec(memory_space=pltpu.VMEM)
    return pl.pallas_call(
        finish_kernel,
        out_shape=jax.ShapeDtypeStruct((128, 512), BF16),
        in_specs=[smem] * 3 + [vmem] * 7,
        out_specs=vmem,
        cost_estimate=pl.CostEstimate(flops=400_000, bytes_accessed=1_500_000, transcendentals=0),
        name="finish",
    )(
        meta,
        eps_occ,
        eps_vir,
        occ_col,
        eps_vir[None, :],
        *parts,
    )


def gather_z(t, early):
    z0 = lax.axis_index("zh") * 4 + lax.axis_index("zl")
    parts = [(0, t)]
    fwd = bwd = t
    for k in range(1, 5):
        fwd = lax.ppermute(fwd, Z, z_shift(1))
        if k == 1:
            fwd, *early = lax.optimization_barrier((fwd, *early))
        parts.append((-k, fwd))
        if k < 4:
            bwd = lax.ppermute(bwd, Z, z_shift(-1))
            parts.append((k, bwd))
    mine = jnp.zeros((8,) + t.shape, t.dtype)
    for d, part in parts:
        z = (z0 + (d & 7)) & 7
        mine = lax.dynamic_update_slice(mine, part[None], ((z & 3) * 2 + (z >> 2), 0, 0))
    return mine, early


def split_rows(ts):
    return [t.reshape(-1, 32, 16, 128) for t in ts]


def local(amplitudes, ladder_ints, tile_live, cycle_direct, cycle_exchange, eps_occ, eps_vir):
    x0, c0, y0 = lax.axis_index("x"), lax.axis_index("core"), lax.axis_index("y")
    meta = jnp.stack([x0, c0, y0, lax.axis_index(C), lax.axis_index(G)]).astype(jnp.int32)
    both = jnp.stack([cycle_direct, cycle_exchange]).reshape(2, 4, 32, 4, 128)
    both = both.transpose(2, 0, 1, 3, 4).reshape(32, 2, 16, 128)
    occ_col = jnp.broadcast_to(eps_occ[:, None], (32, 128))
    mine, (both, occ_col, meta) = gather_z(amplitudes, (both, occ_col, meta))
    down = lax.ppermute(mine, "y", shift(4, 1))
    up = lax.ppermute(mine, "y", shift(4, -1))
    both, mine = lax.optimization_barrier((both, mine))
    both = lax.all_to_all(both, G, 0, 0, tiled=True)
    xs = [both] + [lax.ppermute(both, "x", shift(4, -s)) for s in (1, 2, 3)]
    *xs, down, up = lax.optimization_barrier((*xs, down, up))
    wa = jnp.stack(xs)
    wb = lax.ppermute(wa, "core", shift(2, 1))
    low = lax.ppermute(down[:4], "y", shift(4, 1))
    high = lax.ppermute(up[4:], "y", shift(4, -1))
    first, last = [mine, down, up], [low, high]
    prev = list(ladder_call(FIRST, meta, tile_live, first, split_rows(first), ladder_ints, wa, wb))
    *last, prev[0] = lax.optimization_barrier((*last, prev[0]))
    keep, away = ladder_call(LAST, meta, tile_live, last, split_rows(last), ladder_ints, wa, wb, tuple(prev))
    got = lax.ppermute(away, "core", shift(2, 1))
    parts = [keep[0], got[0]]
    for s in (1, 2, 3):
        parts.append(lax.ppermute(keep[s] + got[s], "x", shift(4, s)))
    return finish_call(meta, occ_col, eps_occ, eps_vir, parts)


def solution(mesh):
    fine = Mesh(mesh.devices.reshape(4, 2, 4, 4, 2), ("zl", "zh", "y", "x", "core"))
    placed = (P(G, C), P(C, G), P(C, G), P(C, G), P(C, G), P(), P())
    return jax.shard_map(local, mesh=fine, in_specs=placed, out_specs=P(C, G), check_vma=False)
```

```python
import functools

import jax
import jax.numpy as jnp
from jax import lax
from jax.experimental import pallas as pl
from jax.experimental.pallas import tpu as pltpu
from jax.sharding import Mesh, PartitionSpec as P

G = ("zl", "zh", "y")
C = ("x", "core")
Z = ("zl", "zh")
F32 = jnp.float32
BF16 = jnp.bfloat16


def shift(n, s):
    return [(i, (i + s) % n) for i in range(n)]


def z_shift(s):
    at = lambda z: (z % 4) * 2 + z // 4
    return [(at(z), at((z + s) % 8)) for z in range(8)]


NEAR = (-2, 5)
FAR = (3, 3)
CUTS = {NEAR: 3, FAR: 1}


def ladder_kernel(group, meta, live, *refs):
    low, n = group
    cut = CUTS[group]
    ts, us, (v, wa, wb), refs = refs[:5], refs[5:10], refs[10:13], refs[13:]
    blocks = [(p, d, q, d) for p, q in ((0, 0), (1, 1)) for d in range(n)]
    blocks += [(2, d, 2, d) for d in range(cut)] + [(3, d - cut, 2, d) for d in range(cut, n)]
    blocks += [(4, d, 3, d) for d in range(n)]
    prev = None
    if group is FAR:
        vm = v
        prev, refs = refs[0], refs[1:]
    outs, (ladder, wm, o2) = refs[:-3], refs[-3:]
    if group is NEAR:
        vm = outs[1]
    x0, c0, y0, col, z0 = meta[0], meta[1], meta[2], meta[3], meta[5]
    ys = [(y0 + 4 - q) & 3 for q in range(4)]
    zs = [(z0 + low + 8 + lax.rem(e + 4 * n - z0, n)) & 7 for e in range(n)]
    hs = [((z & 3) << 1) | (z >> 2) for z in zs]
    at = [((((z >> 2) ^ c0) << 2) | (((z & 3) + 4 - x0) & 3)) for z in zs]

    if group is NEAR:

        @pl.loop(0, 16)
        def _(kt):
            rows = pl.ds(pl.multiple_of(kt * 128, 128), 128)
            for c in range(4):
                cols = slice(c * 128, c * 128 + 128)
                tile = v[rows, cols]
                vm[rows, cols] = jnp.where(live[kt, c] != 0, tile, jnp.zeros_like(tile))

    @pl.loop(0, 8)
    def _(r):
        ladder[r] = jnp.zeros((512, 128), F32) if prev is None else prev[r]

    half = 2 * n
    for part_of in (blocks[:half], blocks[half:]):
        rows = jnp.concatenate([ts[p][e] for p, e, _, _ in part_of], 0)
        part = jnp.dot(rows, vm[...], preferred_element_type=F32)
        for m, (_, _, q, d) in enumerate(part_of):
            for a in range(4):
                rows = pl.ds(ys[q] * 4 + a, 32, stride=16)
                ladder[at[d], rows, :] += part[m * 32 : m * 32 + 32, a * 128 : a * 128 + 128]

    lane = lax.broadcasted_iota(jnp.int32, (128, 128), 1)

    def spread(k, which):
        pieces = [w[s, k, which] for w in (wa, wb) for s in range(4)]
        return jnp.concatenate(pieces, 0)

    acc = jnp.zeros((512, 128), F32)
    w_all = None
    for m in range(0, 4 * n, 2):
        pair = blocks[m : m + 2]
        lhs = jnp.concatenate([us[p][e].reshape(512, 128) for p, e, _, _ in pair], 1)
        rhs = jnp.concatenate([spread(hs[d] * 4 + ys[q], 1) for _, _, q, d in pair], 1)
        acc = acc + lax.dot_general(lhs, rhs, (((1,), (1,)), ((), ())), preferred_element_type=F32)
        if m % 8 == 0:
            w_all = jnp.zeros((128, 128), F32)
        for f, (_, _, q, d) in enumerate(pair):
            place = m % 8 + f
            wk = spread(hs[d] * 4 + ys[q], 0).astype(F32)
            wk = pltpu.roll(wk, (16 * place + 128 - 16 * col) & 127, 1)
            w_all = jnp.where((lane >> 4) == place, wk, w_all)
        if m % 8 == 6 or m + 2 == 4 * n:
            top = m // 8 * 128
            width = min(128, 64 * n - top)
            wm[:, top : top + width] = w_all[:, :width].astype(BF16)
    o2[...] = acc.T

    own = (lane >> 4) == col

    @pl.loop(0, 16)
    def _(jj):
        j = jj * 2
        rhs = jnp.concatenate(
            [jnp.concatenate([us[p][e, j + f] for p, e, _, _ in blocks], 0) for f in range(2)], 1
        )
        one = jnp.dot(wm[...], rhs, preferred_element_type=F32)
        two = o2[:, pl.ds(pl.multiple_of((jj >> 2) * 128, 128), 128)]
        for f in range(2):
            placed = pltpu.roll(two, (16 * col + 128 - 16 * ((j + f) & 7)) & 127, 1)
            both = one[:, f * 128 : f * 128 + 128] + jnp.where(own, placed, 0.0)
            rows = pl.ds(pl.multiple_of((j + f) * 16, 16), 16)
            for r in range(8):
                value = ladder[r, rows, :] + both[r * 16 : r * 16 + 16]
                if prev is None:
                    outs[0][r, rows, :] = value
                else:
                    outs[r // 4][r % 4, rows, :] = value


def ladder_call(group, meta, live, ts, us, v, wa, wb, prev=()):
    smem = pl.BlockSpec(memory_space=pltpu.SMEM)
    vmem = pl.BlockSpec(memory_space=pltpu.VMEM)
    whole = jax.ShapeDtypeStruct((8, 512, 128), F32)
    half = jax.ShapeDtypeStruct((4, 512, 128), F32)
    masked = jax.ShapeDtypeStruct((2048, 512), BF16)
    return pl.pallas_call(
        functools.partial(ladder_kernel, group),
        out_shape=(half, half) if prev else (whole, masked),
        in_specs=[smem, smem] + [vmem] * (13 + len(prev)),
        out_specs=(vmem, vmem),
        scratch_shapes=[
            pltpu.VMEM((8, 512, 128), F32),
            pltpu.VMEM((128, 64 * group[1]), BF16),
            pltpu.VMEM((128, 512), F32),
        ],
        cost_estimate=pl.CostEstimate(flops=400_000_000 * group[1], bytes_accessed=10_000_000, transcendentals=0),
        compiler_params=pltpu.CompilerParams(vmem_limit_bytes=24 << 20),
        name="ladder",
    )(meta, live, *ts, *us, v, wa, wb, *prev)


def finish_kernel(meta, occ, vir, occ_col, vir_row, p0, p1, p2, p3, p4, out):
    col, g = meta[3], meta[4]
    for il in range(4):
        for a in range(4):
            rows = pl.ds(il * 4 + a, 32, stride=16)
            total = ((p0[rows, :] + p1[rows, :]) + p2[rows, :]) + (p3[rows, :] + p4[rows, :])
            denom = ((vir[g * 4 + a] + vir_row[...]) - occ[col * 4 + il]) - occ_col[...]
            out[il * 32 : il * 32 + 32, a * 128 : a * 128 + 128] = (total / denom).astype(BF16)


def finish_call(meta, occ_col, eps_occ, eps_vir, parts):
    smem = pl.BlockSpec(memory_space=pltpu.SMEM)
    vmem = pl.BlockSpec(memory_space=pltpu.VMEM)
    return pl.pallas_call(
        finish_kernel,
        out_shape=jax.ShapeDtypeStruct((128, 512), BF16),
        in_specs=[smem] * 3 + [vmem] * 7,
        out_specs=vmem,
        cost_estimate=pl.CostEstimate(flops=400_000, bytes_accessed=1_500_000, transcendentals=0),
        name="finish",
    )(
        meta,
        eps_occ,
        eps_vir,
        occ_col,
        eps_vir[None, :],
        *parts,
    )


def over_y(group, cut):
    down = lax.ppermute(group, "y", shift(4, 1))
    up = lax.ppermute(group, "y", shift(4, -1))
    first = lax.ppermute(down[:cut], "y", shift(4, 1))
    rest = lax.ppermute(up[cut:], "y", shift(4, -1))
    return [group, down, first, rest, up]


def split_rows(ts):
    return [t.reshape(-1, 32, 16, 128) for t in ts]


def place(buffer, group, z0, d, block):
    low, n = group
    return lax.dynamic_update_slice(buffer, block[None], (lax.rem(z0 + (d - low) % n, n), 0, 0))


def local(amplitudes, ladder_ints, tile_live, cycle_direct, cycle_exchange, eps_occ, eps_vir):
    x0, c0, y0 = lax.axis_index("x"), lax.axis_index("core"), lax.axis_index("y")
    z0 = lax.axis_index("zh") * 4 + lax.axis_index("zl")
    meta = jnp.stack([x0, c0, y0, lax.axis_index(C), lax.axis_index(G), z0]).astype(jnp.int32)
    both = jnp.stack([cycle_direct, cycle_exchange]).reshape(2, 4, 32, 4, 128)
    both = both.transpose(2, 0, 1, 3, 4).reshape(32, 2, 16, 128)
    both = lax.all_to_all(both, G, 0, 0, tiled=True)
    occ_col = jnp.broadcast_to(eps_occ[:, None], (32, 128))
    near = place(jnp.zeros((5, 32, 2048), BF16), NEAR, z0, 0, amplitudes)
    far = jnp.zeros((3, 32, 2048), BF16)
    fwd = bwd = amplitudes
    for k in range(1, 3):
        fwd, bwd = lax.ppermute(fwd, Z, z_shift(1)), lax.ppermute(bwd, Z, z_shift(-1))
        near = place(place(near, NEAR, z0, -k, fwd), NEAR, z0, k, bwd)
    ts_near = over_y(near, CUTS[NEAR])
    xs = [both] + [lax.ppermute(both, "x", shift(4, -s)) for s in (1, 2, 3)]
    fwd, bwd = lax.ppermute(fwd, Z, z_shift(1)), lax.ppermute(bwd, Z, z_shift(-1))
    far = place(place(far, FAR, z0, 5, fwd), FAR, z0, 3, bwd)
    far = place(far, FAR, z0, 4, lax.ppermute(fwd, Z, z_shift(1)))
    ts_far = over_y(far, CUTS[FAR])
    *xs, ts_near[1], ts_near[4], occ_col = lax.optimization_barrier((*xs, ts_near[1], ts_near[4], occ_col))
    wa = jnp.stack(xs)
    wb = lax.ppermute(wa, "core", shift(2, 1))
    *ts_near, wb = lax.optimization_barrier((*ts_near, wb))
    first, masked = ladder_call(NEAR, meta, tile_live, ts_near, split_rows(ts_near), ladder_ints, wa, wb)
    *ts_far, first = lax.optimization_barrier((*ts_far, first))
    keep, away = ladder_call(FAR, meta, tile_live, ts_far, split_rows(ts_far), masked, wa, wb, (first,))
    got = lax.ppermute(away, "core", shift(2, 1))
    parts = [keep[0], got[0]]
    for s in (1, 2, 3):
        parts.append(lax.ppermute(keep[s] + got[s], "x", shift(4, s)))
    return finish_call(meta, occ_col, eps_occ, eps_vir, parts)


def solution(mesh):
    fine = Mesh(mesh.devices.reshape(4, 2, 4, 4, 2), ("zl", "zh", "y", "x", "core"))
    placed = (P(G, C), P(C, G), P(C, G), P(C, G), P(C, G), P(), P())
    return jax.shard_map(local, mesh=fine, in_specs=placed, out_specs=P(C, G), check_vma=False)
```

```python
import functools

import jax
import jax.numpy as jnp
from jax import lax
from jax.experimental import pallas as pl
from jax.experimental.pallas import tpu as pltpu
from jax.sharding import Mesh, PartitionSpec as P

G = ("zl", "zh", "y")
C = ("x", "core")
Z = ("zl", "zh")
F32 = jnp.float32
BF16 = jnp.bfloat16


def shift(n, s):
    return [(i, (i + s) % n) for i in range(n)]


def z_shift(s):
    at = lambda z: (z % 4) * 2 + z // 4
    return [(at(z), at((z + s) % 8)) for z in range(8)]


NEAR = (-2, 5)
FAR = (3, 3)
CUTS = {NEAR: 3, FAR: 1}
FIRST = ((NEAR, 0, 0, 5), (NEAR, 1, 0, 5), (NEAR, 3, 0, 5), (FAR, 0, 0, 3))
LAST = ((FAR, 1, 0, 3), (FAR, 3, 0, 3), (NEAR, 2, 0, 3), (NEAR, 2, 3, 2), (FAR, 2, 0, 1), (FAR, 2, 1, 2))


def ladder_kernel(pieces, meta, live, *refs):
    n = len(pieces)
    ts, us, (v, wa, wb), refs = refs[:n], refs[n : 2 * n], refs[2 * n : 2 * n + 3], refs[2 * n + 3 :]
    prev = None
    if pieces is LAST:
        vm = v
        prev, refs = refs[0], refs[1:]
    outs, (ladder, wm, o2) = refs[:-3], refs[-3:]
    if pieces is FIRST:
        vm = outs[1]
    x0, c0, y0, col, z0 = meta[0], meta[1], meta[2], meta[3], meta[5]
    blocks = []
    for p, ((low, size), q, top, count) in enumerate(pieces):
        for e in range(count):
            z = (z0 + low + 8 + lax.rem(top + e + 4 * size - z0, size)) & 7
            h = ((z & 3) << 1) | (z >> 2)
            spot = (((z >> 2) ^ c0) << 2) | (((z & 3) + 4 - x0) & 3)
            blocks.append((p, e, (y0 + 4 - q) & 3, h, spot))

    if pieces is FIRST:

        @pl.loop(0, 16)
        def _(kt):
            rows = pl.ds(pl.multiple_of(kt * 128, 128), 128)
            for c in range(4):
                cols = slice(c * 128, c * 128 + 128)
                tile = v[rows, cols]
                vm[rows, cols] = jnp.where(live[kt, c] != 0, tile, jnp.zeros_like(tile))

    @pl.loop(0, 8)
    def _(r):
        ladder[r] = jnp.zeros((512, 128), F32) if prev is None else prev[r]

    half = len(blocks) // 2
    for part_of in (blocks[:half], blocks[half:]):
        rows = jnp.concatenate([ts[p][e] for p, e, *_ in part_of], 0)
        part = jnp.dot(rows, vm[...], preferred_element_type=F32)
        for m, (_, _, y, _, spot) in enumerate(part_of):
            for a in range(4):
                rows = pl.ds(y * 4 + a, 32, stride=16)
                ladder[spot, rows, :] += part[m * 32 : m * 32 + 32, a * 128 : a * 128 + 128]

    lane = lax.broadcasted_iota(jnp.int32, (128, 128), 1)

    def spread(k, which):
        pieces = [w[s, k, which] for w in (wa, wb) for s in range(4)]
        return jnp.concatenate(pieces, 0)

    acc = jnp.zeros((512, 128), F32)
    w_all = None
    for m in range(0, len(blocks), 2):
        pair = blocks[m : m + 2]
        lhs = jnp.concatenate([us[p][e].reshape(512, 128) for p, e, *_ in pair], 1)
        rhs = jnp.concatenate([spread(h * 4 + y, 1) for _, _, y, h, _ in pair], 1)
        acc = acc + lax.dot_general(lhs, rhs, (((1,), (1,)), ((), ())), preferred_element_type=F32)
        if m % 8 == 0:
            w_all = jnp.zeros((128, 128), F32)
        for f, (_, _, y, h, _) in enumerate(pair):
            place = m % 8 + f
            wk = spread(h * 4 + y, 0).astype(F32)
            wk = pltpu.roll(wk, (16 * place + 128 - 16 * col) & 127, 1)
            w_all = jnp.where((lane >> 4) == place, wk, w_all)
        if m % 8 == 6 or m + 2 == len(blocks):
            top = m // 8 * 128
            width = min(128, 16 * len(blocks) - top)
            wm[:, top : top + width] = w_all[:, :width].astype(BF16)
    o2[...] = acc.T

    own = (lane >> 4) == col

    @pl.loop(0, 16)
    def _(jj):
        j = jj * 2
        rhs = jnp.concatenate(
            [jnp.concatenate([us[p][e, j + f] for p, e, *_ in blocks], 0) for f in range(2)], 1
        )
        one = jnp.dot(wm[...], rhs, preferred_element_type=F32)
        two = o2[:, pl.ds(pl.multiple_of((jj >> 2) * 128, 128), 128)]
        for f in range(2):
            placed = pltpu.roll(two, (16 * col + 128 - 16 * ((j + f) & 7)) & 127, 1)
            both = one[:, f * 128 : f * 128 + 128] + jnp.where(own, placed, 0.0)
            rows = pl.ds(pl.multiple_of((j + f) * 16, 16), 16)
            for r in range(8):
                value = ladder[r, rows, :] + both[r * 16 : r * 16 + 16]
                if prev is None:
                    outs[0][r, rows, :] = value
                else:
                    outs[r // 4][r % 4, rows, :] = value


def ladder_call(pieces, meta, live, ts, us, v, wa, wb, prev=()):
    smem = pl.BlockSpec(memory_space=pltpu.SMEM)
    vmem = pl.BlockSpec(memory_space=pltpu.VMEM)
    count = sum(piece[3] for piece in pieces)
    whole = jax.ShapeDtypeStruct((8, 512, 128), F32)
    half = jax.ShapeDtypeStruct((4, 512, 128), F32)
    masked = jax.ShapeDtypeStruct((2048, 512), BF16)
    return pl.pallas_call(
        functools.partial(ladder_kernel, pieces),
        out_shape=(half, half) if prev else (whole, masked),
        in_specs=[smem, smem] + [vmem] * (2 * len(pieces) + 3 + len(prev)),
        out_specs=(vmem, vmem),
        scratch_shapes=[
            pltpu.VMEM((8, 512, 128), F32),
            pltpu.VMEM((128, 16 * count), BF16),
            pltpu.VMEM((128, 512), F32),
        ],
        cost_estimate=pl.CostEstimate(flops=100_000_000 * count, bytes_accessed=10_000_000, transcendentals=0),
        compiler_params=pltpu.CompilerParams(vmem_limit_bytes=24 << 20),
        name="ladder",
    )(meta, live, *ts, *us, v, wa, wb, *prev)


def finish_kernel(meta, occ, vir, occ_col, vir_row, p0, p1, p2, p3, p4, out):
    col, g = meta[3], meta[4]
    for il in range(4):
        for a in range(4):
            rows = pl.ds(il * 4 + a, 32, stride=16)
            total = ((p0[rows, :] + p1[rows, :]) + p2[rows, :]) + (p3[rows, :] + p4[rows, :])
            denom = ((vir[g * 4 + a] + vir_row[...]) - occ[col * 4 + il]) - occ_col[...]
            out[il * 32 : il * 32 + 32, a * 128 : a * 128 + 128] = (total / denom).astype(BF16)


def finish_call(meta, occ_col, eps_occ, eps_vir, parts):
    smem = pl.BlockSpec(memory_space=pltpu.SMEM)
    vmem = pl.BlockSpec(memory_space=pltpu.VMEM)
    return pl.pallas_call(
        finish_kernel,
        out_shape=jax.ShapeDtypeStruct((128, 512), BF16),
        in_specs=[smem] * 3 + [vmem] * 7,
        out_specs=vmem,
        cost_estimate=pl.CostEstimate(flops=400_000, bytes_accessed=1_500_000, transcendentals=0),
        name="finish",
    )(
        meta,
        eps_occ,
        eps_vir,
        occ_col,
        eps_vir[None, :],
        *parts,
    )


def beside(group):
    return lax.ppermute(group, "y", shift(4, 1)), lax.ppermute(group, "y", shift(4, -1))


def onward(down, up, cut):
    first = lax.ppermute(down[:cut], "y", shift(4, 1))
    return first, lax.ppermute(up[cut:], "y", shift(4, -1))


def split_rows(ts):
    return [t.reshape(-1, 32, 16, 128) for t in ts]


def place(buffer, group, z0, d, block):
    low, n = group
    return lax.dynamic_update_slice(buffer, block[None], (lax.rem(z0 + (d - low) % n, n), 0, 0))


def local(amplitudes, ladder_ints, tile_live, cycle_direct, cycle_exchange, eps_occ, eps_vir):
    x0, c0, y0 = lax.axis_index("x"), lax.axis_index("core"), lax.axis_index("y")
    z0 = lax.axis_index("zh") * 4 + lax.axis_index("zl")
    meta = jnp.stack([x0, c0, y0, lax.axis_index(C), lax.axis_index(G), z0]).astype(jnp.int32)
    both = jnp.stack([cycle_direct, cycle_exchange]).reshape(2, 4, 32, 4, 128)
    both = both.transpose(2, 0, 1, 3, 4).reshape(32, 2, 16, 128)
    both = lax.all_to_all(both, G, 0, 0, tiled=True)
    occ_col = jnp.broadcast_to(eps_occ[:, None], (32, 128))
    near = place(jnp.zeros((5, 32, 2048), BF16), NEAR, z0, 0, amplitudes)
    far = jnp.zeros((3, 32, 2048), BF16)
    fwd = bwd = amplitudes
    for k in range(1, 3):
        fwd, bwd = lax.ppermute(fwd, Z, z_shift(1)), lax.ppermute(bwd, Z, z_shift(-1))
        near = place(place(near, NEAR, z0, -k, fwd), NEAR, z0, k, bwd)
    near_down, near_up = beside(near)
    xs = [both] + [lax.ppermute(both, "x", shift(4, -s)) for s in (1, 2, 3)]
    fwd, bwd = lax.ppermute(fwd, Z, z_shift(1)), lax.ppermute(bwd, Z, z_shift(-1))
    far = place(place(far, FAR, z0, 5, fwd), FAR, z0, 3, bwd)
    far = place(far, FAR, z0, 4, lax.ppermute(fwd, Z, z_shift(1)))
    far_down, far_up = beside(far)
    *xs, near_down, near_up, occ_col = lax.optimization_barrier((*xs, near_down, near_up, occ_col))
    wa = jnp.stack(xs)
    wb = lax.ppermute(wa, "core", shift(2, 1))
    near_two = onward(near_down, near_up, CUTS[NEAR])
    first = [near, near_down, near_up, far]
    *first, wb = lax.optimization_barrier((*first, wb))
    prev, masked = ladder_call(FIRST, meta, tile_live, first, split_rows(first), ladder_ints, wa, wb)
    far_down, far_up, prev = lax.optimization_barrier((far_down, far_up, prev))
    last = [far_down, far_up, *near_two, *onward(far_down, far_up, CUTS[FAR])]
    keep, away = ladder_call(LAST, meta, tile_live, last, split_rows(last), masked, wa, wb, (prev,))
    got = lax.ppermute(away, "core", shift(2, 1))
    parts = [keep[0], got[0]]
    for s in (1, 2, 3):
        parts.append(lax.ppermute(keep[s] + got[s], "x", shift(4, s)))
    return finish_call(meta, occ_col, eps_occ, eps_vir, parts)


def solution(mesh):
    fine = Mesh(mesh.devices.reshape(4, 2, 4, 4, 2), ("zl", "zh", "y", "x", "core"))
    placed = (P(G, C), P(C, G), P(C, G), P(C, G), P(C, G), P(), P())
    return jax.shard_map(local, mesh=fine, in_specs=placed, out_specs=P(C, G), check_vma=False)
```

```python
import functools

import jax
import jax.numpy as jnp
from jax import lax
from jax.experimental import pallas as pl
from jax.experimental.pallas import tpu as pltpu
from jax.sharding import Mesh, PartitionSpec as P

G = ("zl", "zh", "y")
C = ("x", "core")
Z = ("zl", "zh")
UNROLL = 8
F32 = jnp.float32
BF16 = jnp.bfloat16


def shift(n, s):
    return [(i, (i + s) % n) for i in range(n)]


def z_shift(s):
    at = lambda z: (z % 4) * 2 + z // 4
    return [(at(z), at((z + s) % 8)) for z in range(8)]


NEAR = (-2, 5)
FAR = (3, 3)
CUTS = {NEAR: 3, FAR: 1}
FIRST = ((NEAR, 0, 0, 5), (NEAR, 1, 0, 5), (NEAR, 3, 0, 5), (FAR, 0, 0, 3))
LAST = ((FAR, 1, 0, 3), (FAR, 3, 0, 3), (NEAR, 2, 0, 3), (NEAR, 2, 3, 2), (FAR, 2, 0, 1), (FAR, 2, 1, 2))


def ladder_kernel(pieces, meta, live, *refs):
    n = len(pieces)
    ts, us, (v, wa, wb), refs = refs[:n], refs[n : 2 * n], refs[2 * n : 2 * n + 3], refs[2 * n + 3 :]
    prev = None
    if pieces is LAST:
        vm = v
        prev, refs = refs[0], refs[1:]
    outs, (ladder, wm, o2) = refs[:-3], refs[-3:]
    if pieces is FIRST:
        vm = outs[1]
    x0, c0, y0, col, z0 = meta[0], meta[1], meta[2], meta[3], meta[5]
    blocks = []
    for p, ((low, size), q, top, count) in enumerate(pieces):
        for e in range(count):
            z = (z0 + low + 8 + lax.rem(top + e + 4 * size - z0, size)) & 7
            h = ((z & 3) << 1) | (z >> 2)
            spot = (((z >> 2) ^ c0) << 2) | (((z & 3) + 4 - x0) & 3)
            blocks.append((p, e, (y0 + 4 - q) & 3, h, spot))

    if pieces is FIRST:

        @pl.loop(0, 16, unroll=4)
        def _(kt):
            rows = pl.ds(pl.multiple_of(kt * 128, 128), 128)
            for c in range(4):
                cols = slice(c * 128, c * 128 + 128)
                tile = v[rows, cols]
                vm[rows, cols] = jnp.where(live[kt, c] != 0, tile, jnp.zeros_like(tile))

    @pl.loop(0, 8)
    def _(r):
        ladder[r] = jnp.zeros((512, 128), F32)

    half = len(blocks) // 2
    for part_of in (blocks[:half], blocks[half:]):
        rows = jnp.concatenate([ts[p][e] for p, e, *_ in part_of], 0)
        part = jnp.dot(rows, vm[...], preferred_element_type=F32)
        for m, (_, _, y, _, spot) in enumerate(part_of):
            for a in range(4):
                rows = pl.ds(y * 4 + a, 32, stride=16)
                ladder[spot, rows, :] = part[m * 32 : m * 32 + 32, a * 128 : a * 128 + 128]

    lane = lax.broadcasted_iota(jnp.int32, (128, 128), 1)

    def spread(k, which):
        pieces = [w[s, k, which] for w in (wa, wb) for s in range(4)]
        return jnp.concatenate(pieces, 0)

    acc = jnp.zeros((512, 128), F32)
    w_all = None
    for m in range(0, len(blocks), 2):
        pair = blocks[m : m + 2]
        lhs = jnp.concatenate([us[p][e].reshape(512, 128) for p, e, *_ in pair], 1)
        rhs = jnp.concatenate([spread(h * 4 + y, 1) for _, _, y, h, _ in pair], 1)
        acc = acc + lax.dot_general(lhs, rhs, (((1,), (1,)), ((), ())), preferred_element_type=F32)
        if m % 8 == 0:
            w_all = jnp.zeros((128, 128), F32)
        for f, (_, _, y, h, _) in enumerate(pair):
            place = m % 8 + f
            wk = spread(h * 4 + y, 0).astype(F32)
            wk = pltpu.roll(wk, (16 * place + 128 - 16 * col) & 127, 1)
            w_all = jnp.where((lane >> 4) == place, wk, w_all)
        if m % 8 == 6 or m + 2 == len(blocks):
            top = m // 8 * 128
            width = min(128, 16 * len(blocks) - top)
            wm[:, top : top + width] = w_all[:, :width].astype(BF16)
    o2[...] = acc.T

    own = (lane >> 4) == col

    @pl.loop(0, 16, unroll=UNROLL)
    def _(jj):
        j = jj * 2
        rhs = jnp.concatenate(
            [jnp.concatenate([us[p][e, j + f] for p, e, *_ in blocks], 0) for f in range(2)], 1
        )
        one = jnp.dot(wm[...], rhs, preferred_element_type=F32)
        two = o2[:, pl.ds(pl.multiple_of((jj >> 2) * 128, 128), 128)]
        for f in range(2):
            placed = pltpu.roll(two, (16 * col + 128 - 16 * ((j + f) & 7)) & 127, 1)
            both = one[:, f * 128 : f * 128 + 128] + jnp.where(own, placed, 0.0)
            rows = pl.ds(pl.multiple_of((j + f) * 16, 16), 16)
            for r in range(8):
                value = ladder[r, rows, :] + both[r * 16 : r * 16 + 16]
                if prev is None:
                    outs[0][r, rows, :] = value
                else:
                    outs[r // 4][r % 4, rows, :] = value + prev[r, rows, :]


def ladder_call(pieces, meta, live, ts, us, v, wa, wb, prev=()):
    smem = pl.BlockSpec(memory_space=pltpu.SMEM)
    vmem = pl.BlockSpec(memory_space=pltpu.VMEM)
    count = sum(piece[3] for piece in pieces)
    whole = jax.ShapeDtypeStruct((8, 512, 128), F32)
    half = jax.ShapeDtypeStruct((4, 512, 128), F32)
    masked = jax.ShapeDtypeStruct((2048, 512), BF16)
    return pl.pallas_call(
        functools.partial(ladder_kernel, pieces),
        out_shape=(half, half) if prev else (whole, masked),
        in_specs=[smem, smem] + [vmem] * (2 * len(pieces) + 3 + len(prev)),
        out_specs=(vmem, vmem),
        scratch_shapes=[
            pltpu.VMEM((8, 512, 128), F32),
            pltpu.VMEM((128, 16 * count), BF16),
            pltpu.VMEM((128, 512), F32),
        ],
        cost_estimate=pl.CostEstimate(flops=100_000_000 * count, bytes_accessed=10_000_000, transcendentals=0),
        compiler_params=pltpu.CompilerParams(vmem_limit_bytes=24 << 20),
        name="ladder",
    )(meta, live, *ts, *us, v, wa, wb, *prev)


def finish_kernel(meta, occ, vir, vir_row, p0, p1, p2, p3, p4, out, total):
    col, g = meta[3], meta[4]
    row = lax.broadcasted_iota(jnp.int32, (32, 128), 0)
    occ_col = jnp.zeros((32, 128), F32)
    for j in range(32):
        occ_col = jnp.where(row == j, occ[j], occ_col)
    total[...] = ((p0[...] + p1[...]) + p2[...]) + (p3[...] + p4[...])
    for il in range(4):
        for a in range(4):
            value = total[pl.ds(il * 4 + a, 32, stride=16), :]
            denom = ((vir[g * 4 + a] + vir_row[...]) - occ[col * 4 + il]) - occ_col
            out[il * 32 : il * 32 + 32, a * 128 : a * 128 + 128] = (value / denom).astype(BF16)


def finish_call(meta, eps_occ, eps_vir, parts):
    smem = pl.BlockSpec(memory_space=pltpu.SMEM)
    vmem = pl.BlockSpec(memory_space=pltpu.VMEM)
    return pl.pallas_call(
        finish_kernel,
        out_shape=jax.ShapeDtypeStruct((128, 512), BF16),
        in_specs=[smem] * 3 + [vmem] * 6,
        out_specs=vmem,
        scratch_shapes=[pltpu.VMEM((512, 128), F32)],
        cost_estimate=pl.CostEstimate(flops=400_000, bytes_accessed=1_500_000, transcendentals=0),
        name="finish",
    )(
        meta,
        eps_occ,
        eps_vir,
        eps_vir[None, :],
        *parts,
    )


def beside(group):
    return lax.ppermute(group, "y", shift(4, 1)), lax.ppermute(group, "y", shift(4, -1))


def onward(down, up, cut):
    first = lax.ppermute(down[:cut], "y", shift(4, 1))
    return first, lax.ppermute(up[cut:], "y", shift(4, -1))


def split_rows(ts):
    return [t.reshape(-1, 32, 16, 128) for t in ts]


def place(buffer, group, z0, d, block):
    low, n = group
    return lax.dynamic_update_slice(buffer, block[None], (lax.rem(z0 + (d - low) % n, n), 0, 0))


def local(amplitudes, ladder_ints, tile_live, cycle_direct, cycle_exchange, eps_occ, eps_vir):
    x0, c0, y0 = lax.axis_index("x"), lax.axis_index("core"), lax.axis_index("y")
    z0 = lax.axis_index("zh") * 4 + lax.axis_index("zl")
    meta = jnp.stack([x0, c0, y0, lax.axis_index(C), lax.axis_index(G), z0]).astype(jnp.int32)
    both = jnp.stack([cycle_direct, cycle_exchange]).reshape(2, 4, 32, 4, 128)
    both = both.transpose(2, 0, 1, 3, 4).reshape(32, 2, 16, 128)
    both = lax.all_to_all(both, G, 0, 0, tiled=True)
    near = place(jnp.zeros((5, 32, 2048), BF16), NEAR, z0, 0, amplitudes)
    far = jnp.zeros((3, 32, 2048), BF16)
    fwd = bwd = amplitudes
    for k in range(1, 3):
        fwd, bwd = lax.ppermute(fwd, Z, z_shift(1)), lax.ppermute(bwd, Z, z_shift(-1))
        near = place(place(near, NEAR, z0, -k, fwd), NEAR, z0, k, bwd)
    near_down, near_up = beside(near)
    xs = [both] + [lax.ppermute(both, "x", shift(4, -s)) for s in (1, 2, 3)]
    fwd, bwd = lax.ppermute(fwd, Z, z_shift(1)), lax.ppermute(bwd, Z, z_shift(-1))
    far = place(place(far, FAR, z0, 5, fwd), FAR, z0, 3, bwd)
    far = place(far, FAR, z0, 4, lax.ppermute(fwd, Z, z_shift(1)))
    far_down, far_up = beside(far)
    *xs, near_down, near_up = lax.optimization_barrier((*xs, near_down, near_up))
    wa = jnp.stack(xs)
    wb = lax.ppermute(wa, "core", shift(2, 1))
    near_two = onward(near_down, near_up, CUTS[NEAR])
    first = [near, near_down, near_up, far]
    *first, wb = lax.optimization_barrier((*first, wb))
    prev, masked = ladder_call(FIRST, meta, tile_live, first, split_rows(first), ladder_ints, wa, wb)
    far_down, far_up, prev = lax.optimization_barrier((far_down, far_up, prev))
    last = [far_down, far_up, *near_two, *onward(far_down, far_up, CUTS[FAR])]
    keep, away = ladder_call(LAST, meta, tile_live, last, split_rows(last), masked, wa, wb, (prev,))
    got = lax.ppermute(away, "core", shift(2, 1))
    parts = [keep[0], got[0]]
    for s in (1, 2, 3):
        parts.append(lax.ppermute(keep[s] + got[s], "x", shift(4, s)))
    return finish_call(meta, eps_occ, eps_vir, parts)


def solution(mesh):
    fine = Mesh(mesh.devices.reshape(4, 2, 4, 4, 2), ("zl", "zh", "y", "x", "core"))
    placed = (P(G, C), P(C, G), P(C, G), P(C, G), P(C, G), P(), P())
    return jax.shard_map(local, mesh=fine, in_specs=placed, out_specs=P(C, G), check_vma=False)
```

```python
import functools

import jax
import jax.numpy as jnp
from jax import lax
from jax.experimental import pallas as pl
from jax.experimental.pallas import tpu as pltpu
from jax.sharding import Mesh, PartitionSpec as P

G = ("zl", "zh", "y")
C = ("x", "core")
Z = ("zl", "zh")
UNROLL = 8
F32 = jnp.float32
BF16 = jnp.bfloat16


def shift(n, s):
    return [(i, (i + s) % n) for i in range(n)]


def z_shift(s):
    at = lambda z: (z % 4) * 2 + z // 4
    return [(at(z), at((z + s) % 8)) for z in range(8)]


NEAR = (-2, 5)
FAR = (3, 3)
CUTS = {NEAR: 3, FAR: 1}
FIRST = ((NEAR, 0, 0, 5), (NEAR, 1, 0, 5), (NEAR, 3, 0, 5), (FAR, 0, 0, 3))
LAST = ((FAR, 1, 0, 3), (FAR, 3, 0, 3), (NEAR, 2, 0, 3), (NEAR, 2, 3, 2), (FAR, 2, 0, 1), (FAR, 2, 1, 2))


def ladder_kernel(pieces, meta, live, *refs):
    n = len(pieces)
    ts, us, (v, wa, wb), refs = refs[:n], refs[n : 2 * n], refs[2 * n : 2 * n + 3], refs[2 * n + 3 :]
    prev = None
    if pieces is LAST:
        vm = v
        prev, refs = refs[0], refs[1:]
    outs, (ladder, wm, o2) = refs[:-3], refs[-3:]
    if pieces is FIRST:
        vm = outs[1]
    x0, c0, y0, col, z0 = meta[0], meta[1], meta[2], meta[3], meta[5]
    blocks = []
    for p, ((low, size), q, top, count) in enumerate(pieces):
        for e in range(count):
            z = (z0 + low + 8 + lax.rem(top + e + 4 * size - z0, size)) & 7
            h = ((z & 3) << 1) | (z >> 2)
            spot = (((z >> 2) ^ c0) << 2) | (((z & 3) + 4 - x0) & 3)
            blocks.append((p, e, (y0 + 4 - q) & 3, h, spot))

    if pieces is FIRST:

        @pl.loop(0, 16, unroll=4)
        def _(kt):
            rows = pl.ds(pl.multiple_of(kt * 128, 128), 128)
            for c in range(4):
                cols = slice(c * 128, c * 128 + 128)
                tile = v[rows, cols]
                vm[rows, cols] = jnp.where(live[kt, c] != 0, tile, jnp.zeros_like(tile))

    @pl.loop(0, 8)
    def _(r):
        ladder[r] = jnp.zeros((512, 128), F32)

    half = len(blocks) // 2
    for part_of in (blocks[:half], blocks[half:]):
        rows = jnp.concatenate([ts[p][e] for p, e, *_ in part_of], 0)
        part = jnp.dot(rows, vm[...], preferred_element_type=F32)
        for m, (_, _, y, _, spot) in enumerate(part_of):
            for a in range(4):
                rows = pl.ds(y * 4 + a, 32, stride=16)
                ladder[spot, rows, :] = part[m * 32 : m * 32 + 32, a * 128 : a * 128 + 128]

    lane = lax.broadcasted_iota(jnp.int32, (128, 128), 1)

    def spread(k, which):
        pieces = [w[s, k, which] for w in (wa, wb) for s in range(4)]
        return jnp.concatenate(pieces, 0)

    acc = jnp.zeros((512, 128), F32)
    w_all = None
    for m in range(0, len(blocks), 2):
        pair = blocks[m : m + 2]
        lhs = jnp.concatenate([us[p][e].reshape(512, 128) for p, e, *_ in pair], 1)
        rhs = jnp.concatenate([spread(h * 4 + y, 1) for _, _, y, h, _ in pair], 1)
        acc = acc + lax.dot_general(lhs, rhs, (((1,), (1,)), ((), ())), preferred_element_type=F32)
        if m % 8 == 0:
            w_all = jnp.zeros((128, 128), F32)
        for f, (_, _, y, h, _) in enumerate(pair):
            place = m % 8 + f
            wk = spread(h * 4 + y, 0).astype(F32)
            wk = pltpu.roll(wk, (16 * place + 128 - 16 * col) & 127, 1)
            w_all = jnp.where((lane >> 4) == place, wk, w_all)
        if m % 8 == 6 or m + 2 == len(blocks):
            top = m // 8 * 128
            width = min(128, 16 * len(blocks) - top)
            wm[:, top : top + width] = w_all[:, :width].astype(BF16)
    o2[...] = acc.T

    own = (lane >> 4) == col

    @pl.loop(0, 16, unroll=UNROLL)
    def _(jj):
        j = jj * 2
        rhs = jnp.concatenate(
            [jnp.concatenate([us[p][e, j + f] for p, e, *_ in blocks], 0) for f in range(2)], 1
        )
        one = jnp.dot(wm[...], rhs, preferred_element_type=F32)
        two = o2[:, pl.ds(pl.multiple_of((jj >> 2) * 128, 128), 128)]
        for f in range(2):
            placed = pltpu.roll(two, (16 * col + 128 - 16 * ((j + f) & 7)) & 127, 1)
            both = one[:, f * 128 : f * 128 + 128] + jnp.where(own, placed, 0.0)
            rows = pl.ds(pl.multiple_of((j + f) * 16, 16), 16)
            for r in range(8):
                value = ladder[r, rows, :] + both[r * 16 : r * 16 + 16]
                if prev is None:
                    outs[0][r, rows, :] = value
                else:
                    outs[r // 4][r % 4, rows, :] = value + prev[r, rows, :]


def ladder_call(pieces, meta, live, ts, us, v, wa, wb, prev=()):
    smem = pl.BlockSpec(memory_space=pltpu.SMEM)
    vmem = pl.BlockSpec(memory_space=pltpu.VMEM)
    count = sum(piece[3] for piece in pieces)
    whole = jax.ShapeDtypeStruct((8, 512, 128), F32)
    half = jax.ShapeDtypeStruct((4, 512, 128), F32)
    masked = jax.ShapeDtypeStruct((2048, 512), BF16)
    return pl.pallas_call(
        functools.partial(ladder_kernel, pieces),
        out_shape=(half, half) if prev else (whole, masked),
        in_specs=[smem, smem] + [vmem] * (2 * len(pieces) + 3 + len(prev)),
        out_specs=(vmem, vmem),
        scratch_shapes=[
            pltpu.VMEM((8, 512, 128), F32),
            pltpu.VMEM((128, 16 * count), BF16),
            pltpu.VMEM((128, 512), F32),
        ],
        cost_estimate=pl.CostEstimate(flops=100_000_000 * count, bytes_accessed=10_000_000, transcendentals=0),
        compiler_params=pltpu.CompilerParams(vmem_limit_bytes=24 << 20),
        name="ladder",
    )(meta, live, *ts, *us, v, wa, wb, *prev)


def finish_kernel(meta, occ, vir, vir_row, p0, p1, p2, p3, p4, out, total):
    col, g = meta[3], meta[4]
    row = lax.broadcasted_iota(jnp.int32, (32, 128), 0)
    occ_col = jnp.zeros((32, 128), F32)
    for j in range(32):
        occ_col = jnp.where(row == j, occ[j], occ_col)
    total[...] = ((p0[0] + p1[0]) + p2[...]) + (p3[...] + p4[...])
    for il in range(4):
        for a in range(4):
            value = total[pl.ds(il * 4 + a, 32, stride=16), :]
            denom = ((vir[g * 4 + a] + vir_row[...]) - occ[col * 4 + il]) - occ_col
            out[il * 32 : il * 32 + 32, a * 128 : a * 128 + 128] = (value / denom).astype(BF16)


def finish_call(meta, eps_occ, eps_vir, parts):
    smem = pl.BlockSpec(memory_space=pltpu.SMEM)
    vmem = pl.BlockSpec(memory_space=pltpu.VMEM)
    return pl.pallas_call(
        finish_kernel,
        out_shape=jax.ShapeDtypeStruct((128, 512), BF16),
        in_specs=[smem] * 3 + [vmem] * 6,
        out_specs=vmem,
        scratch_shapes=[pltpu.VMEM((512, 128), F32)],
        cost_estimate=pl.CostEstimate(flops=400_000, bytes_accessed=1_500_000, transcendentals=0),
        name="finish",
    )(
        meta,
        eps_occ,
        eps_vir,
        eps_vir[None, :],
        *parts,
    )


def beside(group):
    return lax.ppermute(group, "y", shift(4, 1)), lax.ppermute(group, "y", shift(4, -1))


def onward(down, up, cut):
    first = lax.ppermute(down[:cut], "y", shift(4, 1))
    return first, lax.ppermute(up[cut:], "y", shift(4, -1))


def split_rows(ts):
    return [t.reshape(-1, 32, 16, 128) for t in ts]


def place(buffer, group, z0, d, block):
    low, n = group
    return lax.dynamic_update_slice(buffer, block[None], (lax.rem(z0 + (d - low) % n, n), 0, 0))


def local(amplitudes, ladder_ints, tile_live, cycle_direct, cycle_exchange, eps_occ, eps_vir):
    x0, c0, y0 = lax.axis_index("x"), lax.axis_index("core"), lax.axis_index("y")
    z0 = lax.axis_index("zh") * 4 + lax.axis_index("zl")
    meta = jnp.stack([x0, c0, y0, lax.axis_index(C), lax.axis_index(G), z0]).astype(jnp.int32)
    both = jnp.stack([cycle_direct, cycle_exchange]).reshape(2, 4, 32, 4, 128)
    both = both.transpose(2, 0, 1, 3, 4).reshape(32, 2, 16, 128)
    near = place(jnp.zeros((5, 32, 2048), BF16), NEAR, z0, 0, amplitudes)
    far = jnp.zeros((3, 32, 2048), BF16)
    fwd = bwd = amplitudes
    for k in range(1, 3):
        fwd, bwd = lax.ppermute(fwd, Z, z_shift(1)), lax.ppermute(bwd, Z, z_shift(-1))
        if k == 1:
            fwd, bwd, both = lax.optimization_barrier((fwd, bwd, both))
            both = lax.all_to_all(both, G, 0, 0, tiled=True)
        near = place(place(near, NEAR, z0, -k, fwd), NEAR, z0, k, bwd)
    near_down, near_up = beside(near)
    xs = [both] + [lax.ppermute(both, "x", shift(4, -s)) for s in (1, 2, 3)]
    fwd, bwd = lax.ppermute(fwd, Z, z_shift(1)), lax.ppermute(bwd, Z, z_shift(-1))
    far = place(place(far, FAR, z0, 5, fwd), FAR, z0, 3, bwd)
    far = place(far, FAR, z0, 4, lax.ppermute(fwd, Z, z_shift(1)))
    far_down, far_up = beside(far)
    *xs, near_down, near_up = lax.optimization_barrier((*xs, near_down, near_up))
    wa = jnp.stack(xs)
    wb = lax.ppermute(wa, "core", shift(2, 1))
    near_two = onward(near_down, near_up, CUTS[NEAR])
    first = [near, near_down, near_up, far]
    *first, wb = lax.optimization_barrier((*first, wb))
    prev, masked = ladder_call(FIRST, meta, tile_live, first, split_rows(first), ladder_ints, wa, wb)
    far_down, far_up, prev = lax.optimization_barrier((far_down, far_up, prev))
    last = [far_down, far_up, *near_two, *onward(far_down, far_up, CUTS[FAR])]
    keep, away = ladder_call(LAST, meta, tile_live, last, split_rows(last), masked, wa, wb, (prev,))
    got = lax.ppermute(away, "core", shift(2, 1))
    parts = [keep, got]
    for s in (1, 2, 3):
        parts.append(lax.ppermute(keep[s] + got[s], "x", shift(4, s)))
    return finish_call(meta, eps_occ, eps_vir, parts)


def solution(mesh):
    fine = Mesh(mesh.devices.reshape(4, 2, 4, 4, 2), ("zl", "zh", "y", "x", "core"))
    placed = (P(G, C), P(C, G), P(C, G), P(C, G), P(C, G), P(), P())
    return jax.shard_map(local, mesh=fine, in_specs=placed, out_specs=P(C, G), check_vma=False)
```

```python
import functools

import jax
import jax.numpy as jnp
from jax import lax
from jax.experimental import pallas as pl
from jax.experimental.pallas import tpu as pltpu
from jax.sharding import Mesh, PartitionSpec as P

G = ("zl", "zh", "y")
C = ("x", "core")
Z = ("zl", "zh")
UNROLL = 8
F32 = jnp.float32
BF16 = jnp.bfloat16


def shift(n, s):
    return [(i, (i + s) % n) for i in range(n)]


def z_shift(s):
    at = lambda z: (z % 4) * 2 + z // 4
    return [(at(z), at((z + s) % 8)) for z in range(8)]


NEAR = (-2, 5)
FAR = (3, 3)
CUTS = {NEAR: 3, FAR: 1}
FIRST = ((NEAR, 0, 0, 5), (NEAR, 1, 0, 5), (NEAR, 3, 0, 5), (FAR, 0, 0, 3))
LAST = ((FAR, 1, 0, 3), (FAR, 3, 0, 3), (NEAR, 2, 0, 3), (NEAR, 2, 3, 2), (FAR, 2, 0, 1), (FAR, 2, 1, 2))


def ladder_kernel(pieces, meta, live, *refs):
    n = len(pieces)
    ts, us, (v, wa, wb), refs = refs[:n], refs[n : 2 * n], refs[2 * n : 2 * n + 3], refs[2 * n + 3 :]
    prev = None
    if pieces is LAST:
        vm = v
        prev, refs = refs[0], refs[1:]
    outs, (ladder, wm, o2) = refs[:-3], refs[-3:]
    if pieces is FIRST:
        vm = outs[1]
    x0, c0, y0, col, z0 = meta[0], meta[1], meta[2], meta[3], meta[5]
    blocks = []
    for p, ((low, size), q, top, count) in enumerate(pieces):
        for e in range(count):
            z = (z0 + low + 8 + lax.rem(top + e + 4 * size - z0, size)) & 7
            h = ((z & 3) << 1) | (z >> 2)
            spot = (((z >> 2) ^ c0) << 2) | (((z & 3) + 4 - x0) & 3)
            blocks.append((p, e, (y0 + 4 - q) & 3, h, spot))

    if pieces is FIRST:

        @pl.loop(0, 16, unroll=4)
        def _(kt):
            rows = pl.ds(pl.multiple_of(kt * 128, 128), 128)
            for c in range(4):
                cols = slice(c * 128, c * 128 + 128)
                tile = v[rows, cols]
                vm[rows, cols] = jnp.where(live[kt, c] != 0, tile, jnp.zeros_like(tile))

    @pl.loop(0, 8)
    def _(r):
        ladder[r] = jnp.zeros((512, 128), F32)

    half = len(blocks) // 2
    for part_of in (blocks[:half], blocks[half:]):
        rows = jnp.concatenate([ts[p][e] for p, e, *_ in part_of], 0)
        part = jnp.dot(rows, vm[...], preferred_element_type=F32)
        for m, (_, _, y, _, spot) in enumerate(part_of):
            for a in range(4):
                rows = pl.ds(y * 4 + a, 32, stride=16)
                ladder[spot, rows, :] = part[m * 32 : m * 32 + 32, a * 128 : a * 128 + 128]

    lane = lax.broadcasted_iota(jnp.int32, (128, 128), 1)

    def spread(k, which):
        pieces = [w[s, k, which] for w in (wa, wb) for s in range(4)]
        return jnp.concatenate(pieces, 0)

    acc = jnp.zeros((512, 128), F32)
    w_all = None
    for m in range(0, len(blocks), 2):
        pair = blocks[m : m + 2]
        lhs = jnp.concatenate([us[p][e].reshape(512, 128) for p, e, *_ in pair], 1)
        rhs = jnp.concatenate([spread(h * 4 + y, 1) for _, _, y, h, _ in pair], 1)
        acc = acc + lax.dot_general(lhs, rhs, (((1,), (1,)), ((), ())), preferred_element_type=F32)
        if m % 8 == 0:
            w_all = jnp.zeros((128, 128), F32)
        for f, (_, _, y, h, _) in enumerate(pair):
            place = m % 8 + f
            wk = spread(h * 4 + y, 0).astype(F32)
            wk = pltpu.roll(wk, (16 * place + 128 - 16 * col) & 127, 1)
            w_all = jnp.where((lane >> 4) == place, wk, w_all)
        if m % 8 == 6 or m + 2 == len(blocks):
            top = m // 8 * 128
            width = min(128, 16 * len(blocks) - top)
            wm[:, top : top + width] = w_all[:, :width].astype(BF16)
    o2[...] = acc.T

    own = (lane >> 4) == col

    @pl.loop(0, 16, unroll=UNROLL)
    def _(jj):
        j = jj * 2
        rhs = jnp.concatenate(
            [jnp.concatenate([us[p][e, j + f] for p, e, *_ in blocks], 0) for f in range(2)], 1
        )
        one = jnp.dot(wm[...], rhs, preferred_element_type=F32)
        two = o2[:, pl.ds(pl.multiple_of((jj >> 2) * 128, 128), 128)]
        for f in range(2):
            placed = pltpu.roll(two, (16 * col + 128 - 16 * ((j + f) & 7)) & 127, 1)
            both = one[:, f * 128 : f * 128 + 128] + jnp.where(own, placed, 0.0)
            rows = pl.ds(pl.multiple_of((j + f) * 16, 16), 16)
            for r in range(8):
                value = ladder[r, rows, :] + both[r * 16 : r * 16 + 16]
                if prev is None:
                    outs[0][r, rows, :] = value
                else:
                    outs[r // 4][r % 4, rows, :] = value + prev[r, rows, :]


def ladder_call(pieces, meta, live, ts, us, v, wa, wb, prev=()):
    smem = pl.BlockSpec(memory_space=pltpu.SMEM)
    vmem = pl.BlockSpec(memory_space=pltpu.VMEM)
    count = sum(piece[3] for piece in pieces)
    whole = jax.ShapeDtypeStruct((8, 512, 128), F32)
    half = jax.ShapeDtypeStruct((4, 512, 128), F32)
    masked = jax.ShapeDtypeStruct((2048, 512), BF16)
    return pl.pallas_call(
        functools.partial(ladder_kernel, pieces),
        out_shape=(half, half) if prev else (whole, masked),
        in_specs=[smem, smem] + [vmem] * (2 * len(pieces) + 3 + len(prev)),
        out_specs=(vmem, vmem),
        scratch_shapes=[
            pltpu.VMEM((8, 512, 128), F32),
            pltpu.VMEM((128, 16 * count), BF16),
            pltpu.VMEM((128, 512), F32),
        ],
        cost_estimate=pl.CostEstimate(flops=100_000_000 * count, bytes_accessed=10_000_000, transcendentals=0),
        compiler_params=pltpu.CompilerParams(vmem_limit_bytes=24 << 20),
        name="ladder",
    )(meta, live, *ts, *us, v, wa, wb, *prev)


def finish_kernel(meta, occ, vir, vir_row, p0, p1, p2, p3, p4, out, total):
    col, g = meta[3], meta[4]
    row = lax.broadcasted_iota(jnp.int32, (32, 128), 0)
    occ_col = jnp.zeros((32, 128), F32)
    for j in range(32):
        occ_col = jnp.where(row == j, occ[j], occ_col)
    total[...] = ((p0[0] + p1[0]) + p2[...]) + (p3[...] + p4[...])
    for il in range(4):
        for a in range(4):
            value = total[pl.ds(il * 4 + a, 32, stride=16), :]
            denom = ((vir[g * 4 + a] + vir_row[...]) - occ[col * 4 + il]) - occ_col
            out[il * 32 : il * 32 + 32, a * 128 : a * 128 + 128] = (value / denom).astype(BF16)


def finish_call(meta, eps_occ, eps_vir, parts):
    smem = pl.BlockSpec(memory_space=pltpu.SMEM)
    vmem = pl.BlockSpec(memory_space=pltpu.VMEM)
    return pl.pallas_call(
        finish_kernel,
        out_shape=jax.ShapeDtypeStruct((128, 512), BF16),
        grid=(1,),
        in_specs=[smem] * 3 + [vmem] + [pl.BlockSpec((1, 512, 128), lambda n: (0, 0, 0))] * 2 + [vmem] * 3,
        out_specs=vmem,
        scratch_shapes=[pltpu.VMEM((512, 128), F32)],
        cost_estimate=pl.CostEstimate(flops=400_000, bytes_accessed=1_500_000, transcendentals=0),
        name="finish",
    )(
        meta,
        eps_occ,
        eps_vir,
        eps_vir[None, :],
        *parts,
    )


def beside(group):
    return lax.ppermute(group, "y", shift(4, 1)), lax.ppermute(group, "y", shift(4, -1))


def onward(down, up, cut):
    first = lax.ppermute(down[:cut], "y", shift(4, 1))
    return first, lax.ppermute(up[cut:], "y", shift(4, -1))


def split_rows(ts):
    return [t.reshape(-1, 32, 16, 128) for t in ts]


def place(buffer, group, z0, d, block):
    low, n = group
    return lax.dynamic_update_slice(buffer, block[None], (lax.rem(z0 + (d - low) % n, n), 0, 0))


def local(amplitudes, ladder_ints, tile_live, cycle_direct, cycle_exchange, eps_occ, eps_vir):
    x0, c0, y0 = lax.axis_index("x"), lax.axis_index("core"), lax.axis_index("y")
    z0 = lax.axis_index("zh") * 4 + lax.axis_index("zl")
    meta = jnp.stack([x0, c0, y0, lax.axis_index(C), lax.axis_index(G), z0]).astype(jnp.int32)
    both = jnp.stack([cycle_direct, cycle_exchange]).reshape(2, 4, 32, 4, 128)
    both = both.transpose(2, 0, 1, 3, 4).reshape(32, 2, 16, 128)
    near = place(jnp.zeros((5, 32, 2048), BF16), NEAR, z0, 0, amplitudes)
    far = jnp.zeros((3, 32, 2048), BF16)
    fwd = bwd = amplitudes
    for k in range(1, 3):
        fwd, bwd = lax.ppermute(fwd, Z, z_shift(1)), lax.ppermute(bwd, Z, z_shift(-1))
        if k == 1:
            fwd, bwd, both = lax.optimization_barrier((fwd, bwd, both))
            both = lax.all_to_all(both, G, 0, 0, tiled=True)
        near = place(place(near, NEAR, z0, -k, fwd), NEAR, z0, k, bwd)
    near_down, near_up = beside(near)
    xs = [both] + [lax.ppermute(both, "x", shift(4, -s)) for s in (1, 2, 3)]
    fwd, bwd = lax.ppermute(fwd, Z, z_shift(1)), lax.ppermute(bwd, Z, z_shift(-1))
    far = place(place(far, FAR, z0, 5, fwd), FAR, z0, 3, bwd)
    far = place(far, FAR, z0, 4, lax.ppermute(fwd, Z, z_shift(1)))
    far_down, far_up = beside(far)
    *xs, near_down, near_up = lax.optimization_barrier((*xs, near_down, near_up))
    wa = jnp.stack(xs)
    wb = lax.ppermute(wa, "core", shift(2, 1))
    near_two = onward(near_down, near_up, CUTS[NEAR])
    first = [near, near_down, near_up, far]
    *first, wb = lax.optimization_barrier((*first, wb))
    prev, masked = ladder_call(FIRST, meta, tile_live, first, split_rows(first), ladder_ints, wa, wb)
    far_down, far_up, prev = lax.optimization_barrier((far_down, far_up, prev))
    last = [far_down, far_up, *near_two, *onward(far_down, far_up, CUTS[FAR])]
    keep, away = ladder_call(LAST, meta, tile_live, last, split_rows(last), masked, wa, wb, (prev,))
    got = lax.ppermute(away, "core", shift(2, 1))
    parts = [keep, got]
    for s in (1, 2, 3):
        parts.append(lax.ppermute(keep[s] + got[s], "x", shift(4, s)))
    return finish_call(meta, eps_occ, eps_vir, parts)


def solution(mesh):
    fine = Mesh(mesh.devices.reshape(4, 2, 4, 4, 2), ("zl", "zh", "y", "x", "core"))
    placed = (P(G, C), P(C, G), P(C, G), P(C, G), P(C, G), P(), P())
    return jax.shard_map(local, mesh=fine, in_specs=placed, out_specs=P(C, G), check_vma=False)
```
